32 devices in a mesh: gx: 2 (over y), gy: 4 (over z), gz: 4 (over x, core).
Axes of the slice: x: 2, y: 2, z: 4, core: 2. Of those that a mesh axis runs over, the one named last changes fastest.
Arguments:
- atom_cell: int32 [3, 8192], P(None, ('gx', 'gy', 'gz')), may hold values from 0 to 63, as said below
- atom_frac: bfloat16 [3, 8192], P(None, ('gx', 'gy', 'gz')), may hold values from 0 to 1
- features: bfloat16 [128, 8192], P(None, ('gx', 'gy', 'gz')), may hold values from -6 to 6
- ghost_export: int32 [2048], P(('gx', 'gy', 'gz')), may hold values from 0 to 255, as said below
- neighbors: int32 [8192, 32], P(('gx', 'gy', 'gz')), may hold values from 0 to 1983, as said below
- neighbor_count: int32 [8192], P(('gx', 'gy', 'gz')), may hold values from 16 to 32
- w_up: bfloat16 [128, 128], replicated, may hold values from -0.5 to 0.5
- radial_weight: float32 [128, 8], replicated, may hold values from -2 to 2
- w_out: bfloat16 [128, 128], replicated, may hold values from -0.5 to 0.5
- energy_weight: bfloat16 [128], replicated, may hold values from -0.5 to 0.5
- charge_weight: bfloat16 [128], replicated, may hold values from -0.5 to 0.5
Outputs:
- forces: float32 [3, 8192], P(None, ('gx', 'gy', 'gz'))
- atom_energy: float32 [8192], P(('gx', 'gy', 'gz'))
The draws below stay inside these ranges and needn't reach their ends.
Inputs may be any that keep to these rules, and one draw needn't show every extreme that they name: `atom_cell`: every atom whose cell is the first or one of the last two along some dimension of its domain is in its domain's ghost_export list. `ghost_export`: 64 distinct local atom indices of each domain. `neighbors`: each row names distinct entries of its domain's table, never the atom itself and never slot 13. Only the first neighbor_count entries of a row are neighbours.
All inputs are finite; a program needn't handle non-finite values.
Results may differ from the reference program's by a relative error of at most 0.0025.
Values may be sent and summed in bfloat16 or wider, within the bound.
No kernel may reach another device: no remote copies, remote signals or barrier semaphores. Data moves between devices by JAX's collectives and lax.ppermute only.
A program may use at most 64 MiB of HBM per device.

```python
import math
import jax
import jax.numpy as jnp
from jax import lax

CHANNELS = 128
RADIAL = 8
NEIGHBORS = 32
BLOCK = 128
CX = 8
CY = 16
CZ = 64
ATOM_DEV = 256
EXPORT_DEV = 64
ATOMS = 8192
GX = 16
GY = 64
GZ = 256
N_GX = 2
N_GY = 4
N_GZ = 4


def shuffle_atoms(sub_key):
    return jax.random.permutation(sub_key, ATOM_DEV)


def atom_layout(key):
    count_x = GX // CX
    count_y = GY // CY
    count_z = GZ // CZ
    device_count = count_x * count_y * count_z
    base_key = jax.random.fold_in(key, 911)
    order_key, free_key, inner_key = jax.random.split(base_key, 3)
    orders = jax.vmap(shuffle_atoms)(jax.random.split(order_key, device_count)).astype(jnp.int32)
    export = orders[:, :EXPORT_DEV]
    ranks = jnp.argsort(orders, axis=1, stable=True)
    free_atom = ranks < EXPORT_DEV
    extents = jnp.array([CX, CY, CZ], jnp.int32)
    free_cells = jax.random.randint(free_key, (3, device_count, ATOM_DEV), 0, extents[:, None, None])
    inner_cells = jax.random.randint(inner_key, (3, device_count, ATOM_DEV), 1, extents[:, None, None] - 2)
    cells = jnp.where(free_atom[None], free_cells, inner_cells).astype(jnp.int32)
    return (cells, export.astype(jnp.int32))


def draw_atom_cell(key, part):
    cells, export = atom_layout(key)
    return cells.reshape(3, -1)


def draw_ghost_export(key, part):
    cells, export = atom_layout(key)
    return export.reshape(-1)


def draw_neighbors(key, part):
    cells, export = atom_layout(key)
    count_x = GX // CX
    count_y = GY // CY
    count_z = GZ // CZ
    device_count = count_x * count_y * count_z
    table_rows = ATOM_DEV + 27 * EXPORT_DEV
    devices = jnp.arange(device_count, dtype=jnp.int32)
    coord_x = devices // (count_y * count_z)
    coord_y = devices // count_z % count_y
    coord_z = devices % count_z
    slot_index = jnp.arange(27, dtype=jnp.int32)
    step_x = slot_index // 9 - 1
    step_y = slot_index // 3 % 3 - 1
    step_z = slot_index % 3 - 1
    partner = ((coord_x[:, None] + step_x[None]) % count_x * count_y + (coord_y[:, None] + step_y[None]) % count_y) * count_z + (coord_z[:, None] + step_z[None]) % count_z
    ghost_cells = cells[:, partner[:, :, None], export[partner]]
    slot_shift = jnp.stack([step_x * CX, step_y * CY, step_z * CZ])
    ghost_cells = ghost_cells + slot_shift[:, None, :, None]
    table = jnp.concatenate([cells, ghost_cells.reshape(3, device_count, 27 * EXPORT_DEV)], axis=2)
    salt_key = jax.random.fold_in(jax.random.fold_in(key, 911), 5)
    salts = jax.random.randint(salt_key, (device_count, ATOM_DEV), 0, table_rows)
    column = jnp.arange(table_rows, dtype=jnp.int32)
    blocked = jnp.logical_and(column >= ATOM_DEV + 13 * EXPORT_DEV, column < ATOM_DEV + 14 * EXPORT_DEV)

    def choose(device):
        own_cells = table[:, device, :ATOM_DEV]
        candidates = table[:, device, :]
        offsets = own_cells[:, :, None] - candidates[:, None, :]
        distance_sq = jnp.sum(offsets * offsets, axis=0)
        noise = (column[None, :] * 7919 + salts[device][:, None]) % table_rows
        score = distance_sq * table_rows + noise
        self_hit = column[None, :] == jnp.arange(ATOM_DEV, dtype=jnp.int32)[:, None]
        score = jnp.where(jnp.logical_or(self_hit, blocked[None, :]), 2 ** 30, score)
        return lax.top_k(-score, NEIGHBORS)[1]
    chosen = lax.map(choose, devices)
    return chosen.reshape(device_count * ATOM_DEV, NEIGHBORS).astype(jnp.int32)


def touch_ends(entries, own_key, low, high):
    shape = entries.shape
    place = [jax.random.randint(jax.random.fold_in(own_key, axis), (), 0, shape[axis]) for axis in range(len(shape))]
    entries = entries.at[tuple(place)].set(low)
    longest = shape.index(max(shape))
    place[longest] = (place[longest] + 1) % shape[longest]
    return entries.at[tuple(place)].set(high)


def steps_of(own_key, shape, shards, smallest, largest):
    gain = 1.0
    for dim, blocks in shards:
        heights = jax.random.uniform(jax.random.fold_in(jax.random.fold_in(own_key, 6), dim), (blocks,), jnp.float32, smallest / len(shards), largest / len(shards))
        gain = gain * jnp.repeat(jnp.exp(heights), shape[dim] // blocks).reshape((-1,) + (1,) * (len(shape) - 1 - dim))
    return gain


def bell_draw(rng, shape, spread, most, shards=(), kind=jnp.bfloat16):
    gain = steps_of(rng, shape, shards, -0.22, 0.18) if shards else 1.0
    result = jax.random.normal(rng, shape, jnp.float32) * spread * gain
    return jnp.minimum(jnp.maximum(result, -most), most).astype(kind)


def setup_inputs(seed: int = 0) -> dict:
    streams_of = jax.random.split(jax.random.key(seed), 12)
    return {
        "atom_cell": draw_atom_cell(jax.random.fold_in(streams_of[11], 71), 0),
        "atom_frac": jnp.clip(1.0 * jax.random.uniform(streams_of[1], (3, ATOMS), jnp.float32) ** steps_of(streams_of[1], (3, ATOMS), ((1, 32),), -0.2, 0.2), 0.0, 1.0).astype(jnp.bfloat16),
        "features": bell_draw(streams_of[2], (CHANNELS, ATOMS), 1.0, 6.0, ((1, 32),)),
        "ghost_export": draw_ghost_export(jax.random.fold_in(streams_of[11], 71), 0),
        "neighbors": draw_neighbors(jax.random.fold_in(streams_of[11], 71), 0),
        "neighbor_count": touch_ends(jax.random.randint(streams_of[5], (ATOMS,), NEIGHBORS // 2, NEIGHBORS + 1), jax.random.fold_in(streams_of[5], 1), NEIGHBORS // 2, NEIGHBORS).astype(jnp.int32),
        "w_up": bell_draw(streams_of[6], (CHANNELS, CHANNELS), CHANNELS ** -0.5, 0.5),
        "radial_weight": bell_draw(streams_of[7], (CHANNELS, RADIAL), RADIAL ** -0.5, 2.0, (), jnp.float32),
        "w_out": bell_draw(streams_of[8], (CHANNELS, CHANNELS), CHANNELS ** -0.5, 0.5),
        "energy_weight": bell_draw(streams_of[9], (CHANNELS,), CHANNELS ** -0.5, 0.5),
        "charge_weight": bell_draw(streams_of[10], (CHANNELS,), CHANNELS ** -0.5, 0.5),
    }


basis_step = 1.4
basis_width = 1.4
message_scale = 0.125
vector_scale = 1.0 / 6.0
ewald_beta_sq = 2.0

def spline_weights(fraction):
    remain = 1.0 - fraction
    squared = fraction * fraction
    cubed = squared * fraction
    return (remain * remain * remain / 6.0, (3.0 * cubed - 6.0 * squared + 4.0) / 6.0, (-3.0 * cubed + 3.0 * squared + 3.0 * fraction + 1.0) / 6.0, cubed / 6.0)

def block_energy(pos_table, up_table, centre_pos, centre_feat, neighbor_block, count_block, radial_weight, w_out, energy_weight):
    row_slots = neighbor_block.shape[1]
    atoms_block = neighbor_block.shape[0]
    flat_index = neighbor_block.T.reshape(-1)
    partner_pos = jnp.take(pos_table, flat_index, axis=1).reshape(3, row_slots, atoms_block)
    relative = partner_pos - centre_pos[:, None, :]
    distance = jnp.sqrt(lax.optimization_barrier(jnp.sum(relative * relative, axis=0)) + 1.0)
    valid_mask = (jnp.arange(row_slots)[:, None] < count_block[None, :]).astype(jnp.float32)
    centres = jnp.arange(radial_weight.shape[1]).astype(jnp.float32) * basis_step
    basis_values = jnp.exp(-jnp.square((distance[None] - centres[:, None, None]) / basis_width)) * valid_mask[None]
    radial = jnp.dot(radial_weight, basis_values.reshape(basis_values.shape[0], -1), precision=lax.Precision.HIGHEST, preferred_element_type=jnp.float32).reshape(-1, row_slots, atoms_block)
    partner_feat = jnp.take(up_table, flat_index, axis=1).reshape(-1, row_slots, atoms_block)
    message = radial * partner_feat.astype(jnp.float32)
    scalar = lax.optimization_barrier(jnp.sum(message, axis=1)) * message_scale
    vector = jnp.einsum('ckn,akn->acn', message, relative, precision=lax.Precision.HIGHEST) * (message_scale * vector_scale)
    invariant = scalar + scalar * scalar + lax.optimization_barrier(jnp.sum(vector * vector, axis=0))
    update = jnp.dot(w_out, invariant.astype(jnp.bfloat16), preferred_element_type=jnp.float32)
    hidden = centre_feat.astype(jnp.float32) + update
    return lax.optimization_barrier(jnp.sum(energy_weight.astype(jnp.float32)[:, None] * jax.nn.silu(hidden), axis=0))

def wave_number(indices, extent):
    folded = (indices + extent // 2) % extent - extent // 2
    return folded.astype(jnp.float32) * (2.0 * math.pi / extent)

def influence_of(wave_x, wave_y, wave_z, cells_total):
    square = wave_x[:, None, None] ** 2 + wave_y[None, :, None] ** 2 + wave_z[None, None, :] ** 2
    positive = square > 0.0
    safe_square = jnp.where(positive, square, 1.0)
    return jnp.where(positive, 4.0 * math.pi / cells_total * jnp.exp(-square / (4.0 * ewald_beta_sq)) / safe_square, 0.0)

def reference(atom_cell, atom_frac, features, ghost_export, neighbors, neighbor_count, w_up, radial_weight, w_out, energy_weight, charge_weight):
    device_count = N_GX * N_GY * N_GZ
    per_device = ATOM_DEV
    exported = EXPORT_DEV
    devices = jnp.arange(device_count, dtype=jnp.int32)
    coord_x = devices // (N_GY * N_GZ)
    coord_y = devices // N_GZ % N_GY
    coord_z = devices % N_GZ
    slot_index = jnp.arange(27, dtype=jnp.int32)
    step_x = slot_index // 9 - 1
    step_y = slot_index // 3 % 3 - 1
    step_z = slot_index % 3 - 1
    partner_device = ((coord_x[:, None] + step_x[None]) % N_GX * N_GY + (coord_y[:, None] + step_y[None]) % N_GY) * N_GZ + (coord_z[:, None] + step_z[None]) % N_GZ
    export_global = ghost_export.reshape(device_count, exported) + (devices * per_device)[:, None]
    ghost_global = export_global[partner_device]
    lookup = jnp.concatenate([devices[:, None] * per_device + jnp.arange(per_device, dtype=jnp.int32)[None, :], ghost_global.reshape(device_count, 27 * exported)], axis=1).astype(jnp.int32)
    slot_shift = jnp.stack([step_x * CX, step_y * CY, step_z * CZ]).astype(jnp.float32)
    shift_table = jnp.concatenate([jnp.zeros((3, per_device), jnp.float32), jnp.repeat(slot_shift, exported, axis=1)], axis=1)
    cell_float = atom_cell.astype(jnp.float32)
    up_all = jnp.dot(w_up, features, preferred_element_type=jnp.float32).astype(jnp.bfloat16)
    charges = jnp.dot(charge_weight, features, preferred_element_type=jnp.float32)

    def short_energy(fraction):
        positions = cell_float + fraction

        def device_energy(device):
            row_ids = lookup[device]
            pos_table = jnp.take(positions, row_ids, axis=1) + shift_table
            up_table = jnp.take(up_all, row_ids, axis=1)

            def one_block(number):
                first_row = (device * per_device + number * BLOCK).astype(jnp.int32)
                return block_energy(pos_table, up_table, lax.dynamic_slice_in_dim(positions, first_row, BLOCK, 1), lax.dynamic_slice_in_dim(features, first_row, BLOCK, 1), lax.dynamic_slice_in_dim(neighbors, first_row, BLOCK, 0), lax.dynamic_slice_in_dim(neighbor_count, first_row, BLOCK, 0), radial_weight, w_out, energy_weight)
            return lax.map(one_block, jnp.arange(per_device // BLOCK, dtype=jnp.int32)).reshape(-1)
        return lax.map(jax.checkpoint(device_energy), devices).reshape(-1)
    anchor_x = jnp.repeat(coord_x * CX, per_device)
    anchor_y = jnp.repeat(coord_y * CY, per_device)
    anchor_z = jnp.repeat(coord_z * CZ, per_device)
    node_x = atom_cell[0] + anchor_x - 1
    node_y = atom_cell[1] + anchor_y - 1
    node_z = atom_cell[2] + anchor_z - 1
    influence = influence_of(wave_number(jnp.arange(GX), GX), wave_number(jnp.arange(GY), GY), wave_number(jnp.arange(GZ), GZ), GX * GY * GZ)

    def long_energy(fraction, charge_values):
        weights = spline_weights(fraction)
        density = jnp.zeros((GX, GY, GZ), jnp.float32)
        for step_one in range(4):
            for step_two in range(4):
                for step_three in range(4):
                    amount = charge_values * weights[step_one][0] * weights[step_two][1] * weights[step_three][2]
                    density = density.at[(node_x + step_one) % GX, (node_y + step_two) % GY, (node_z + step_three) % GZ].add(amount)
        spectrum = jnp.fft.fftn(density)
        power = spectrum.real ** 2 + spectrum.imag ** 2
        return 0.5 * jnp.sum(influence * power)

    def total_energy(fraction, charge_values):
        atom_short = short_energy(fraction)
        return (jnp.sum(atom_short) + long_energy(fraction, charge_values), atom_short)
    (energy_total, atom_short), (grad_frac, grad_charge) = jax.value_and_grad(total_energy, argnums=(0, 1), has_aux=True)(atom_frac.astype(jnp.float32), charges)
    forces = -grad_frac
    atom_energy = atom_short + 0.5 * charges * grad_charge
    return (forces, atom_energy)
```

```python
import functools
import math

import jax
import jax.numpy as jnp
import numpy as np
from jax import lax
from jax.experimental import pallas as pl
from jax.experimental.pallas import tpu as pltpu
from jax.sharding import PartitionSpec as P

CX = 8
CY = 16
CZ = 64
XL = CX + 3
YL = CY + 8
ZL = CZ + 16

basis_step = 1.4
basis_width = 1.4
message_scale = 0.125
vector_scale = 1.0 / 6.0
ewald_beta_sq = 2.0

F32 = jnp.float32
BF16 = jnp.bfloat16
VMEM = pl.BlockSpec(memory_space=pltpu.VMEM)
SMEM = pl.BlockSpec(memory_space=pltpu.SMEM)
PARAMS = pltpu.CompilerParams(vmem_limit_bytes=56 * 1024 * 1024)


def iota(shape, dim):
    return lax.broadcasted_iota(jnp.int32, shape, dim)


def mm(a, b):
    return jnp.dot(a, b, preferred_element_type=F32)


def mm_nt(a, b):
    return lax.dot_general(a, b, (((1,), (1,)), ((), ())), preferred_element_type=F32)


def mm_tn(a, b):
    return lax.dot_general(a, b, (((0,), (0,)), ((), ())), preferred_element_type=F32)


def split2(values):
    high = values.astype(BF16)
    return high, (values - high.astype(F32)).astype(BF16)


def stack3(values):
    high, low = split2(values)
    return jnp.concatenate([high, low, high], axis=0)


def prep_kernel(feat_ref, cell_ref, frac_ref, export_ref, w_up_ref, cw_ref, rec_ref, own_ref, pq_ref, p16_ref):
    channels, atoms = feat_ref.shape
    half = channels // 2
    exported = export_ref.shape[1]
    feat = feat_ref[...]
    up = mm(w_up_ref[...], feat).astype(BF16)
    charge = mm(jnp.broadcast_to(cw_ref[...], (16, channels)), feat)[0:1]
    cell = cell_ref[...].astype(F32)
    frac = frac_ref[...].astype(F32)
    p16_ref[...] = jnp.zeros_like(p16_ref)
    p16_ref[0:3] = cell
    p16_ref[8:11] = frac
    pq_ref[...] = jnp.zeros_like(pq_ref)
    pq_ref[0:3] = cell + frac
    pq_ref[3:4] = charge
    p16 = p16_ref[...].astype(BF16)
    own_ref[0:channels] = up
    own_ref[channels : channels + 16] = p16
    export = export_ref[...]
    twice = jnp.concatenate([export, export], axis=1)
    pick = jnp.where(iota((atoms, 2 * exported), 0) == twice, 1.0, 0.0).astype(BF16)
    first = mm(up[0:half], pick)
    second = mm(up[half:channels], pick)
    left = iota((half, 2 * exported), 1) < exported
    rec_ref[0:half] = jnp.where(left, first, second).astype(BF16)
    rec_ref[half : half + 16] = mm(p16, pick).astype(BF16)


def short_kernel(
    steps,
    before_ref,
    mid_ref,
    after_ref,
    own_ref,
    nbr_ref,
    count_ref,
    pq_ref,
    feat_ref,
    rw_ref,
    rwt_ref,
    w_out_ref,
    ew_ref,
    partner_ref,
    send_ref,
    gown_ref,
    eshort_ref,
    table_ref,
    hot_ref,
    upg_ref,
    msg_ref,
    rel_ref,
    bas_ref,
    sv_ref,
    hi_ref,
    lo_ref,
    acc_ref,
):
    per_axis, x_of = steps
    channels, atoms = feat_ref.shape
    half = channels // 2
    slots = nbr_ref.shape[0]
    rows = channels + 16
    width = table_ref.shape[1]
    blocks = table_ref.shape[0] // rows
    tiles = width // 128
    own_tiles = atoms // 128
    arrays = (before_ref, mid_ref, after_ref)
    exported = 64

    def place(tile):
        block, part = divmod(tile, tiles)
        return block * rows, part * 128

    offsets = [(a, b, c) for a in (-1, 0, 1) for b in (-1, 0, 1) for c in (-1, 0, 1) if (a, b, c) != (0, 0, 0)]
    table_ref[...] = jnp.zeros_like(table_ref)
    for tile in range(own_tiles):
        r, l = place(tile)
        table_ref[r : r + rows, l : l + 128] = own_ref[:, tile * 128 : (tile + 1) * 128]
    left64 = iota((half, 128), 1) < exported
    left16 = iota((16, 128), 1) < exported
    row16 = iota((16, 128), 0)
    for u in range(len(offsets) // 2):
        even, odd = offsets[2 * u], offsets[2 * u + 1]
        e = arrays[even[2] + 1][(even[1] + 1) * per_axis + x_of[even[0] + 1]].astype(F32)
        o = arrays[odd[2] + 1][(odd[1] + 1) * per_axis + x_of[odd[0] + 1]].astype(F32)
        r, l = place(own_tiles + u)
        low = jnp.where(left64, e[0:half], pltpu.roll(o[0:half], 64, 1))
        high = jnp.where(left64, pltpu.roll(e[0:half], 64, 1), o[0:half])
        pos = jnp.where(left16, e[half : half + 16], o[half : half + 16])
        for axis, extent in enumerate((CX, CY, CZ)):
            shift = jnp.where(left16, float(even[axis] * extent), float(odd[axis] * extent))
            pos = pos + jnp.where(row16 == axis, shift, 0.0)
        table_ref[r : r + half, l : l + 128] = low.astype(BF16)
        table_ref[r + half : r + channels, l : l + 128] = high.astype(BF16)
        table_ref[r + channels : r + rows, l : l + 128] = pos.astype(BF16)

    index = nbr_ref[...]
    index = jnp.where(index >= atoms + 13 * exported, index - exported, index)
    hi_ref[...] = index // width
    lo_ref[...] = index % width

    row8 = iota((8, atoms), 0)
    own_pos = jnp.where(row8 < 3, pq_ref[...], 0.0)
    count = count_ref[...]
    centres = iota((8, atoms), 0).astype(F32) * basis_step
    table_row = iota((width, atoms), 0)
    rw_hi, rw_lo = split2(rw_ref[...])
    rw3 = jnp.concatenate([rw_hi.astype(F32), rw_hi.astype(F32), rw_lo.astype(F32), jnp.zeros((channels, 8), F32)], axis=1).astype(BF16)

    def gather(k, carry):
        low = lo_ref[pl.ds(k, 1), :]
        high = hi_ref[pl.ds(k, 1), :]
        hot = jnp.where(table_row == low, 1.0, 0.0).astype(BF16)
        hot_ref[k] = hot
        got = mm(table_ref[...], hot)
        value = got[0:rows]
        for block in range(1, blocks):
            value = jnp.where(high == block, got[block * rows : (block + 1) * rows], value)
        up = value[0:channels]
        upg_ref[k] = up.astype(BF16)
        rel = value[channels : channels + 8] + value[channels + 8 : channels + 16] - own_pos
        dist = jnp.sqrt(jnp.sum(rel * rel, axis=0, keepdims=True) + 1.0)
        rel_ref[k] = jnp.where(row8 == 3, dist, rel)
        scaled = (dist - centres) * (1.0 / basis_width)
        basis = jnp.where(k < count, jnp.exp(-(scaled * scaled)), 0.0)
        bas_ref[k] = basis
        b_hi = basis.astype(BF16).astype(F32)
        b_lo = basis - b_hi
        stacked = jnp.concatenate([b_hi, b_lo, b_hi, jnp.zeros_like(b_hi)], axis=0).astype(BF16)
        msg_ref[k] = mm(rw3, stacked) * up
        return carry

    lax.fori_loop(0, slots, gather, 0, unroll=4)

    part = 16

    def gather_sums(block, carry):
        at = pl.ds(pl.multiple_of(block * part, part), part)
        sums = [jnp.zeros((part, atoms), F32) for _ in range(4)]
        for k in range(slots):
            message = msg_ref[k, at, :]
            sums[0] = sums[0] + message
            for axis in range(3):
                sums[axis + 1] = sums[axis + 1] + message * rel_ref[k, axis : axis + 1, :]
        for axis in range(4):
            sv_ref[axis, at, :] = sums[axis]
        return carry

    lax.fori_loop(0, channels // part, gather_sums, 0)

    scalar = sv_ref[0] * message_scale
    vectors = [sv_ref[axis + 1] * (message_scale * vector_scale) for axis in range(3)]
    invariant = scalar + scalar * scalar + (vectors[0] * vectors[0] + vectors[1] * vectors[1] + vectors[2] * vectors[2])
    w_out = w_out_ref[...]
    hidden = feat_ref[...].astype(F32) + mm(w_out, invariant.astype(BF16))
    ew = ew_ref[...].astype(F32)
    gate = 1.0 / (1.0 + jnp.exp(-hidden))
    eshort_ref[...] = jnp.sum(ew * (hidden * gate), axis=0, keepdims=True)
    d_hidden = ew * (gate * (1.0 + hidden * (1.0 - gate)))
    dh_hi, dh_lo = split2(d_hidden)
    d_inv = (mm_tn(w_out, dh_hi) + mm_tn(w_out, dh_lo)).astype(BF16).astype(F32)
    sv_ref[0] = d_inv * (1.0 + 2.0 * scalar) * message_scale
    for axis in range(3):
        sv_ref[axis + 1] = d_inv * vectors[axis] * (2.0 * message_scale * vector_scale)

    acc_ref[...] = jnp.zeros_like(acc_ref)
    rwt_hi, rwt_lo = split2(rwt_ref[...])
    rwt2 = jnp.concatenate([rwt_hi.astype(F32), rwt_lo.astype(F32)], axis=0).astype(BF16)
    chunk = 32

    def scatter(k, total):
        rel8 = rel_ref[k]
        basis = bas_ref[k]
        dist = rel8[3:4]
        turns = [jnp.zeros((8, atoms), F32) for _ in range(3)]
        q_hi, q_lo = [], []
        for first in range(0, channels, chunk):
            at = slice(first, first + chunk)
            message = msg_ref[k, at, :]
            pull = sv_ref[0, at, :]
            for axis in range(3):
                side = sv_ref[axis + 1, at, :]
                pull = pull + side * rel8[axis : axis + 1]
                turn = side * message
                for r in range(0, chunk, 8):
                    turns[axis] = turns[axis] + turn[r : r + 8]
            high, low = split2(pull * upg_ref[k, at, :].astype(F32))
            q_hi.append(high)
            q_lo.append(low)
        two = mm(rwt2, jnp.concatenate(q_hi, axis=0))
        d_basis = two[0:8] + two[8:16] + mm(rwt2, jnp.concatenate(q_lo, axis=0))[0:8]
        slope = d_basis * basis * ((dist - centres) * (-2.0 / (basis_width * basis_width)))
        d_dist = jnp.sum(slope, axis=0, keepdims=True) / dist
        d_rel = jnp.where(row8 < 3, d_dist * rel8, 0.0)
        for axis in range(3):
            d_rel = d_rel + jnp.where(row8 == axis, jnp.sum(turns[axis], axis=0, keepdims=True), 0.0)
        d_hi = d_rel.astype(BF16).astype(F32)
        both = d_hi + pltpu.roll(d_rel - d_hi, 4, 0)
        high = hi_ref[pl.ds(k, 1), :]
        left = jnp.concatenate([jnp.where(high == block, both, 0.0) for block in range(blocks)], axis=0)
        acc_ref[...] += mm_nt(left.astype(BF16), hot_ref[k])
        return total + d_rel

    total = lax.fori_loop(0, slots, scatter, jnp.zeros((8, atoms), F32), unroll=2)

    def grad_tile(tile):
        block, piece = divmod(tile, tiles)
        g = acc_ref[block * 8 : block * 8 + 8, piece * 128 : (piece + 1) * 128]
        return g + pltpu.roll(g, 4, 0)

    for tile in range(own_tiles):
        gown_ref[:, tile * 128 : (tile + 1) * 128] = grad_tile(tile) - total[:, tile * 128 : (tile + 1) * 128]

    base = 4 * atoms
    info = [pq_ref[r : r + 1, :] for r in range(4)]

    def fill(device, carry):
        for r in range(4):
            send_ref[device, :, r * atoms : (r + 1) * atoms] = info[r]
        send_ref[device, :, base : base + 256] = jnp.zeros((1, 256), F32)
        return carry

    lax.fori_loop(0, send_ref.shape[0], fill, 0)
    left1 = iota((1, 128), 1) < 64
    for u in range(len(offsets) // 2):
        g = grad_tile(own_tiles + u)
        swapped = pltpu.roll(g, 64, 1)
        for side in range(2):
            a, b, c = offsets[2 * u + side]
            device = partner_ref[(a + 1) * 9 + (b + 1) * 3 + c + 1]
            here, there = (g, swapped) if side == 0 else (swapped, g)
            top = jnp.where(left1, here[0:1], there[1:2])
            bottom = jnp.where(left1, here[2:3], 0.0)
            send_ref[device, :, base : base + 128] += top
            send_ref[device, :, base + 128 : base + 256] += bottom


def spline(distance):
    outer = jnp.maximum(2.0 - distance, 0.0)
    inner = jnp.maximum(1.0 - distance, 0.0)
    return outer * outer * outer * (1.0 / 6.0) - inner * inner * inner * (4.0 / 6.0)


def weights_of(count, position):
    gap = (iota((count, position.shape[1]), 0) - 1).astype(F32) - position
    return spline(jnp.abs(gap))


def slopes_of(count, position):
    gap = (iota((count, position.shape[1]), 0) - 1).astype(F32) - position
    distance = jnp.abs(gap)
    outer = jnp.maximum(2.0 - distance, 0.0)
    inner = jnp.maximum(1.0 - distance, 0.0)
    size = outer * outer * 0.5 - inner * inner * 2.0
    return jnp.where(gap > 0.0, size, -size)


def long_kernel(
    counts,
    recv_ref,
    gown_ref,
    eshort_ref,
    pq_ref,
    export_ref,
    hy_ref,
    hzh_ref,
    hzl_ref,
    kx_ref,
    kxo_ref,
    hyo_ref,
    hzoh_ref,
    hzol_ref,
    influence_ref,
    forces_ref,
    energy_ref,
    rho_ref,
    wzh_ref,
    wzl_ref,
    plane_ref,
    spec_ref,
    back_ref,
    phi_ref,
):
    count_x, count_y, count_z = counts
    grid_x, grid_y, grid_z = CX * count_x, CY * count_y, CZ * count_z
    atoms = pq_ref.shape[1]
    tall = grid_y + 8
    rho_ref[...] = jnp.zeros_like(rho_ref)
    wzh_ref[...] = jnp.zeros_like(wzh_ref)
    wzl_ref[...] = jnp.zeros_like(wzl_ref)

    def spread(group, carry):
        for l in range(count_z):
            info = recv_ref[group * count_z + l]
            lanes = slice(l * atoms, (l + 1) * atoms)
            wx = weights_of(16, info[:, 0:atoms]) * info[:, 3 * atoms : 4 * atoms]
            wy = weights_of(YL, info[:, atoms : 2 * atoms])
            high, low = split2(weights_of(ZL, info[:, 2 * atoms : 3 * atoms]))
            inside = min(ZL, grid_z - l * CZ)
            wzh_ref[l * CZ : l * CZ + inside, lanes] = high[0:inside]
            wzl_ref[l * CZ : l * CZ + inside, lanes] = low[0:inside]
            if inside < ZL:
                wzh_ref[0 : ZL - inside, lanes] = high[inside:ZL]
                wzl_ref[0 : ZL - inside, lanes] = low[inside:ZL]
            for x in range(XL):
                plane_ref[x * YL : (x + 1) * YL, lanes] = wx[x : x + 1] * wy
        high, low = split2(plane_ref[...])
        wzh = wzh_ref[...]
        grown = mm_nt(high, wzh) + mm_nt(high, wzl_ref[...]) + mm_nt(low, wzh)
        first = (group // count_y * CX) * tall + (group % count_y) * CY
        for x in range(XL):
            at = pl.ds(pl.multiple_of(first + x * tall, 8), YL)
            rho_ref[at, :] += grown[x * YL : (x + 1) * YL]
        return carry

    lax.fori_loop(0, count_x * count_y, spread, 0)
    for x in range(3):
        rho_ref[x * tall : (x + 1) * tall] += rho_ref[(grid_x + x) * tall : (grid_x + x + 1) * tall]

    def times_z(values, high_ref, low_ref):
        high, low = split2(values)
        table = high_ref[...]
        return mm(high, table) + mm(high, low_ref[...]) + mm(low, table)

    def along_yz(x, carry):
        start = pl.multiple_of(x * tall, 8)
        top = rho_ref[pl.ds(start, 8), :] + rho_ref[pl.ds(start + grid_y, 8), :]
        values = jnp.concatenate([top, rho_ref[pl.ds(start + 8, grid_y - 8), :]], axis=0)
        turned = mm(hy_ref[...], stack3(values))
        spec_ref[pl.ds(pl.multiple_of(x * grid_y, 8), grid_y), :] = times_z(turned, hzh_ref, hzl_ref)
        return carry

    lax.fori_loop(0, grid_x, along_yz, 0, unroll=4)

    def along_x(octet, carry):
        def part(ref, x):
            return ref[pl.ds(pl.multiple_of(x * grid_y + octet * 8, 8), 8), :]

        values = jnp.concatenate([part(spec_ref, x) for x in range(grid_x)], axis=0)
        factor = jnp.concatenate([part(influence_ref, x) for x in range(grid_x)], axis=0)
        back = mm(kxo_ref[...], stack3(mm(kx_ref[...], stack3(values)) * factor))
        for x in range(XL):
            back_ref[pl.ds(pl.multiple_of(x * grid_y + octet * 8, 8), 8), :] = back[x * 8 : (x + 1) * 8]
        return carry

    lax.fori_loop(0, grid_y // 8, along_x, 0, unroll=2)

    for x in range(XL):
        turned = mm(hyo_ref[...], stack3(back_ref[x * grid_y : (x + 1) * grid_y]))
        phi_ref[x * YL : (x + 1) * YL] = times_z(turned, hzoh_ref, hzol_ref)[0:YL]

    own = pq_ref[...]
    charge = own[3:4]
    wx, dx = weights_of(16, own[0:1]), slopes_of(16, own[0:1])
    wy, dy = weights_of(YL, own[1:2]), slopes_of(YL, own[1:2])
    wzh, wzl = split2(jnp.concatenate([weights_of(128, own[2:3]), slopes_of(128, own[2:3])], axis=1))
    high, low = split2(phi_ref[...])
    lines = mm(high, wzh) + mm(high, wzl) + mm(low, wzh)
    potential = jnp.zeros((1, atoms), F32)
    field = [jnp.zeros((1, atoms), F32) for _ in range(3)]
    for x in range(XL):
        flat = lines[x * YL : (x + 1) * YL, 0:atoms]
        steep = lines[x * YL : (x + 1) * YL, atoms : 2 * atoms]
        s0 = jnp.sum(wy * flat, axis=0, keepdims=True)
        sy = jnp.sum(dy * flat, axis=0, keepdims=True)
        sz = jnp.sum(wy * steep, axis=0, keepdims=True)
        here = wx[x : x + 1]
        potential = potential + here * s0
        field[0] = field[0] + dx[x : x + 1] * s0
        field[1] = field[1] + here * sy
        field[2] = field[2] + here * sz
    energy_ref[...] = eshort_ref[...] + 0.5 * charge * potential

    base = 4 * atoms

    def returned(device, sums):
        return sums + recv_ref[device, :, base : base + 256]

    sums = lax.fori_loop(0, recv_ref.shape[0], returned, jnp.zeros((1, 256), F32), unroll=8)
    row8 = iota((8, 128), 0)
    lines3 = (sums[:, 0:128], pltpu.roll(jnp.broadcast_to(sums[:, 0:128], (8, 128)), 64, 1), sums[:, 128:256])
    lent = jnp.zeros((8, 128), F32)
    for axis in range(3):
        lent = jnp.where(row8 == axis, lines3[axis], lent)
    lent = jnp.where(iota((8, 128), 1) < 64, lent, 0.0)
    hot = jnp.where(iota((export_ref.shape[0], atoms), 1) == export_ref[...], 1.0, 0.0)
    hot = jnp.concatenate([hot, jnp.zeros((128 - export_ref.shape[0], atoms), F32)], axis=0).astype(BF16)
    high, low = split2(lent)
    rest = (lent - high.astype(F32) - low.astype(F32)).astype(BF16)
    back = mm(high, hot) + mm(low, hot) + mm(rest, hot)
    for axis in range(3):
        total = charge * field[axis] + gown_ref[axis : axis + 1] + back[axis : axis + 1]
        forces_ref[axis : axis + 1] = -total


def cas_table(extent):
    indices = np.arange(extent)
    angle = (indices[:, None] * indices[None, :] % extent) * (2.0 * np.pi / extent)
    return (np.cos(angle) + np.sin(angle)) / np.sqrt(extent)


def halves(table):
    high = np.asarray(table, np.float32).astype(BF16)
    low = (np.asarray(table, np.float64) - high.astype(np.float64)).astype(np.float32).astype(BF16)
    return high, low


def wide(table):
    high, low = halves(table)
    return np.concatenate([high, high, low], axis=-1)


def wave_squares(extent):
    folded = (np.arange(extent) + extent // 2) % extent - extent // 2
    return (folded * (2.0 * np.pi / extent)) ** 2


def exchange(block, axis):
    size = lax.axis_size(axis)
    up = [(i, (i + 1) % size) for i in range(size)]
    if size <= 2:
        other = lax.ppermute(block, axis, up)
        return other, other
    return lax.ppermute(block, axis, up), lax.ppermute(block, axis, [(j, i) for i, j in up])


def per_device(
    atom_cell,
    atom_frac,
    features,
    ghost_export,
    neighbors,
    neighbor_count,
    w_up,
    radial_weight,
    w_out,
    energy_weight,
    charge_weight,
):
    channels, atoms = features.shape
    exported = ghost_export.shape[0]
    slots = neighbors.shape[1]
    counts = tuple(lax.axis_size(axis) for axis in ("gx", "gy", "gz"))
    count_x, count_y, count_z = counts
    places = tuple(lax.axis_index(axis) for axis in ("gx", "gy", "gz"))
    devices = count_x * count_y * count_z
    half = channels // 2
    rows = channels + 16

    record, own, pq = pl.pallas_call(
        prep_kernel,
        out_shape=(
            jax.ShapeDtypeStruct((half + 16, 2 * exported), BF16),
            jax.ShapeDtypeStruct((rows, atoms), BF16),
            jax.ShapeDtypeStruct((8, atoms), F32),
        ),
        in_specs=[VMEM] * 6,
        out_specs=(VMEM,) * 3,
        scratch_shapes=[pltpu.VMEM((16, atoms), F32)],
        name="prep",
    )(features, atom_cell, atom_frac, ghost_export[None, :], w_up, charge_weight[None, :])

    block = record[None]
    below, above = exchange(block, "gx")
    if count_x <= 2:
        block = jnp.concatenate([block, below], axis=0)
        x_of = (1, 0, 1)
    else:
        block = jnp.concatenate([below, block, above], axis=0)
        x_of = (0, 1, 2)
    per_axis = block.shape[0]
    below, above = exchange(block, "gy")
    block = jnp.concatenate([below, block, above], axis=0)
    below, above = exchange(block, "gz")

    slot = np.arange(27)
    partner = (
        (places[0] + (slot // 9 - 1)) % count_x * count_y + (places[1] + (slot // 3 % 3 - 1)) % count_y
    ) * count_z + (places[2] + (slot % 3 - 1)) % count_z

    width = 512
    blocks = -(-(atoms + 26 * exported) // width)
    payload = 4 * atoms + 256
    send, gown, eshort = pl.pallas_call(
        functools.partial(short_kernel, (per_axis, x_of)),
        out_shape=(
            jax.ShapeDtypeStruct((devices, 1, payload), F32),
            jax.ShapeDtypeStruct((8, atoms), F32),
            jax.ShapeDtypeStruct((1, atoms), F32),
        ),
        in_specs=[VMEM] * 12 + [SMEM],
        out_specs=(VMEM,) * 3,
        scratch_shapes=[
            pltpu.VMEM((blocks * rows, width), BF16),
            pltpu.VMEM((slots, width, atoms), BF16),
            pltpu.VMEM((slots, channels, atoms), BF16),
            pltpu.VMEM((slots, channels, atoms), F32),
            pltpu.VMEM((slots, 8, atoms), F32),
            pltpu.VMEM((slots, 8, atoms), F32),
            pltpu.VMEM((4, channels, atoms), F32),
            pltpu.VMEM((slots, atoms), jnp.int32),
            pltpu.VMEM((slots, atoms), jnp.int32),
            pltpu.VMEM((blocks * 8, width), F32),
        ],
        compiler_params=PARAMS,
        name="short",
    )(
        below,
        block,
        above,
        own,
        neighbors.T,
        neighbor_count[None, :],
        pq,
        features,
        radial_weight,
        radial_weight.T,
        w_out,
        energy_weight[:, None],
        partner.astype(jnp.int32),
    )

    recv = lax.all_to_all(send, ("gx", "gy", "gz"), split_axis=0, concat_axis=0, tiled=True)

    grid_x, grid_y, grid_z = CX * count_x, CY * count_y, CZ * count_z
    cas_x, cas_y, cas_z = cas_table(grid_x), cas_table(grid_y), cas_table(grid_z)
    square = (
        wave_squares(grid_x)[:, None, None] + wave_squares(grid_y)[None, :, None] + wave_squares(grid_z)[None, None, :]
    )
    safe = np.where(square > 0.0, square, 1.0)
    influence = np.where(square > 0.0, 4.0 * math.pi * np.exp(-square / (4.0 * ewald_beta_sq)) / safe, 0.0)
    influence = influence.reshape(grid_x * grid_y, grid_z).astype(np.float32)
    eye = np.eye(8)
    kx = wide(np.kron(cas_x, eye))
    x_rows = (np.arange(count_x)[:, None] * CX + np.arange(XL + 1)[None, :]) % grid_x
    kxo = np.stack([wide(np.kron(cas_x[r], eye)) for r in x_rows])
    y_rows = (np.arange(count_y)[:, None] * CY + np.arange(32)[None, :]) % grid_y
    hyo = np.stack([wide(cas_y[r]) for r in y_rows])
    z_rows = (np.arange(count_z)[:, None] * CZ + np.arange(128)[None, :]) % grid_z
    hzo = [halves(cas_z[:, r] * (np.arange(128) < ZL)[None, :]) for r in z_rows]
    hzoh, hzol = np.stack([t[0] for t in hzo]), np.stack([t[1] for t in hzo])
    hzh, hzl = halves(cas_z)

    def mine(table, place):
        return lax.dynamic_index_in_dim(jnp.asarray(table), place, 0, keepdims=False)

    forces, energy = pl.pallas_call(
        functools.partial(long_kernel, counts),
        out_shape=(jax.ShapeDtypeStruct((3, atoms), F32), jax.ShapeDtypeStruct((1, atoms), F32)),
        in_specs=[VMEM] * 14,
        out_specs=(VMEM,) * 2,
        scratch_shapes=[
            pltpu.VMEM(((grid_x + 3) * (grid_y + 8), grid_z), F32),
            pltpu.VMEM((grid_z, count_z * atoms), BF16),
            pltpu.VMEM((grid_z, count_z * atoms), BF16),
            pltpu.VMEM((XL * YL, count_z * atoms), F32),
            pltpu.VMEM((grid_x * grid_y, grid_z), F32),
            pltpu.VMEM((XL * grid_y, grid_z), F32),
            pltpu.VMEM((XL * YL, 128), F32),
        ],
        compiler_params=PARAMS,
        name="long",
    )(
        recv,
        gown,
        eshort,
        pq,
        ghost_export[:, None],
        jnp.asarray(wide(cas_y)),
        jnp.asarray(hzh),
        jnp.asarray(hzl),
        jnp.asarray(kx),
        mine(kxo, places[0]),
        mine(hyo, places[1]),
        mine(hzoh, places[2]),
        mine(hzol, places[2]),
        jnp.asarray(influence),
    )
    return (forces, energy.reshape(-1))


def solution(mesh):
    spread = ("gx", "gy", "gz")
    in_specs = (
        P(None, spread),
        P(None, spread),
        P(None, spread),
        P(spread),
        P(spread, None),
        P(spread),
        P(),
        P(),
        P(),
        P(),
        P(),
    )
    out_specs = (P(None, spread), P(spread))
    return jax.shard_map(per_device, mesh=mesh, in_specs=in_specs, out_specs=out_specs, check_vma=False)
```

```python
import functools
import math

import jax
import jax.numpy as jnp
import numpy as np
from jax import lax
from jax.experimental import pallas as pl
from jax.experimental.pallas import tpu as pltpu
from jax.sharding import PartitionSpec as P

CX = 8
CY = 16
CZ = 64
XL = CX + 3
YL = CY + 8
YW = CY + 4
ZL = CZ + 16

basis_step = 1.4
basis_width = 1.4
message_scale = 0.125
vector_scale = 1.0 / 6.0
ewald_beta_sq = 2.0

F32 = jnp.float32
BF16 = jnp.bfloat16
VMEM = pl.BlockSpec(memory_space=pltpu.VMEM)
MESH_AXES = ("gx", "gy", "gz")
PARAMS = pltpu.CompilerParams(vmem_limit_bytes=56 * 1024 * 1024)


def iota(shape, dim):
    return lax.broadcasted_iota(jnp.int32, shape, dim)


def mm(a, b):
    return jnp.dot(a, b, preferred_element_type=F32)


def mm_nt(a, b):
    return lax.dot_general(a, b, (((1,), (1,)), ((), ())), preferred_element_type=F32)


def mm_tn(a, b):
    return lax.dot_general(a, b, (((0,), (0,)), ((), ())), preferred_element_type=F32)


def split2(values):
    high = values.astype(BF16)
    return high, (values - high.astype(F32)).astype(BF16)


def stack3(values):
    high, low = split2(values)
    return jnp.concatenate([high, low, high], axis=0)


def prep_kernel(feat_ref, cell_ref, frac_ref, export_ref, w_up_ref, cw_ref, rec_ref, own_ref, pq_ref, info_ref, p16_ref):
    channels, atoms = feat_ref.shape
    half = channels // 2
    exported = export_ref.shape[1]
    feat = feat_ref[...]
    up = mm(w_up_ref[...], feat).astype(BF16)
    charge = mm(jnp.broadcast_to(cw_ref[...], (16, channels)), feat)[0:1]
    cell = cell_ref[...].astype(F32)
    frac = frac_ref[...].astype(F32)
    p16_ref[...] = jnp.zeros_like(p16_ref)
    p16_ref[0:3] = cell
    p16_ref[8:11] = frac
    pq_ref[...] = jnp.zeros_like(pq_ref)
    pq_ref[0:3] = cell + frac
    pq_ref[3:4] = charge
    p16 = p16_ref[...].astype(BF16)
    own_ref[0:channels] = up
    own_ref[channels : channels + 16] = p16
    export = export_ref[...]
    twice = jnp.concatenate([export, export], axis=1)
    pick = jnp.where(iota((atoms, 2 * exported), 0) == twice, 1.0, 0.0).astype(BF16)
    first = mm(up[0:half], pick)
    second = mm(up[half:channels], pick)
    left = iota((half, 2 * exported), 1) < exported
    rec_ref[0:half] = jnp.where(left, first, second).astype(BF16)
    rec_ref[half : half + 16] = mm(p16, pick).astype(BF16)
    info = [pq_ref[r : r + 1, :] for r in range(4)]

    def fill(device, carry):
        for r in range(4):
            info_ref[device, :, r * atoms : (r + 1) * atoms] = info[r]
        return carry

    lax.fori_loop(0, info_ref.shape[0], fill, 0, unroll=8)


def lent_domains(count_x):
    around = [(b, c) for b in (-1, 0, 1) for c in (-1, 0, 1)]
    if count_x <= 2:
        return [(0, b, c) for b, c in around if (b, c) != (0, 0)] + [(1, b, c) for b, c in around]
    return [(a, b, c) for a in (-1, 0, 1) for b, c in around if (a, b, c) != (0, 0, 0)]


def short_kernel(
    setup,
    before_ref,
    mid_ref,
    after_ref,
    own_ref,
    nbr_ref,
    count_ref,
    pq_ref,
    feat_ref,
    rwt_ref,
    w_out_ref,
    ew_ref,
    send_ref,
    gown_ref,
    eshort_ref,
    table_ref,
    lanes_ref,
    hot_ref,
    upg_ref,
    msg_ref,
    rel_ref,
    bas_ref,
    sv_ref,
    shift_ref,
    col_ref,
    acc_ref,
):
    counts, x_of, exported, dense = setup
    count_x = counts[0]
    places = [lax.axis_index(axis) for axis in MESH_AXES]
    channels, atoms = feat_ref.shape
    half = channels // 2
    slots = nbr_ref.shape[0]
    width = table_ref.shape[1]
    blocks = table_ref.shape[0] // dense
    tiles = width // 128
    own_tiles = atoms // 128
    sparse = channels - dense
    all_tiles = lanes_ref.shape[1] // 128
    arrays = (before_ref, mid_ref, after_ref)
    per_axis = mid_ref.shape[0] // 3
    domains = lent_domains(count_x)

    def put(tile, up, pos):
        block, part = divmod(tile, tiles)
        lanes = slice(part * 128, (part + 1) * 128)
        table_ref[block * dense : (block + 1) * dense, lanes] = up[0:dense].astype(BF16)
        lanes = slice(tile * 128, (tile + 1) * 128)
        lanes_ref[0:sparse, lanes] = up[dense:channels]
        lanes_ref[sparse : sparse + 8, lanes] = pos

    last = blocks * tiles
    for tile in range(all_tiles, last):
        block, part = divmod(tile, tiles)
        table_ref[block * dense : (block + 1) * dense, part * 128 : (part + 1) * 128] = jnp.zeros((dense, 128), BF16)
    for tile in range(own_tiles):
        lanes = slice(tile * 128, (tile + 1) * 128)
        both = own_ref[:, lanes].astype(F32)
        put(tile, both[0:channels], both[channels : channels + 8] + both[channels + 8 : channels + 16])
    left64 = iota((half, 128), 1) < exported
    left16 = iota((16, 128), 1) < exported
    left8 = iota((8, 128), 1) < exported
    row8 = iota((8, 128), 0)
    for u in range(all_tiles - own_tiles):
        even = domains[2 * u]
        odd = domains[2 * u + 1] if 2 * u + 1 < len(domains) else None

        def record(domain):
            return arrays[domain[2] + 1][(domain[1] + 1) * per_axis + x_of[domain[0] + 1]].astype(F32)

        e = record(even)
        o = record(odd) if odd else jnp.zeros_like(e)
        odd = odd or (0, 0, 0)
        low = jnp.where(left64, e[0:half], pltpu.roll(o[0:half], 64, 1))
        high = jnp.where(left64, pltpu.roll(e[0:half], 64, 1), o[0:half])
        pos = jnp.where(left16, e[half : half + 16], o[half : half + 16])
        pos = pos[0:8] + pos[8:16]
        for axis, extent in ((1, CY), (2, CZ)):
            shift = jnp.where(left8, float(even[axis] * extent), float(odd[axis] * extent))
            pos = pos + jnp.where(row8 == axis, shift, 0.0)
        put(own_tiles + u, jnp.concatenate([low, high], axis=0), pos)

    index = nbr_ref[...]
    rank = index - atoms
    row = 9 * exported
    if count_x <= 2:
        inner = rank - row
        inner = jnp.where(inner >= 5 * exported, inner - exported, inner)
        outer = jnp.where(rank < row, rank, rank - 2 * row) + 8 * exported
        place = jnp.where(jnp.logical_and(rank >= row, rank < 2 * row), inner, outer)
    else:
        place = jnp.where(rank >= 14 * exported, rank - exported, rank)
    col_ref[...] = jnp.where(rank < 0, index, place + atoms)
    ahead = jnp.where(rank < row, -float(CX), jnp.where(rank < 2 * row, 0.0, float(CX)))
    shift_ref[...] = jnp.where(rank < 0, 0.0, ahead)

    row8 = iota((8, atoms), 0)
    own_pos = jnp.where(row8 < 3, pq_ref[...], 0.0)
    count = count_ref[...]
    centres = iota((8, atoms), 0).astype(F32) * basis_step
    table_row = iota((width, atoms), 0).astype(jnp.int16)
    rwt = rwt_ref[...]
    rwt_hi, rwt_lo = split2(rwt)
    rw3 = jnp.concatenate([rwt_hi.astype(F32), rwt_hi.astype(F32), rwt_lo.astype(F32), jnp.zeros_like(rwt)], axis=0)
    rw3 = jnp.transpose(jnp.concatenate([rw3, jnp.zeros((96, channels), F32)], axis=0))[:, 0:32].astype(BF16)

    def gather(k, carry):
        col = col_ref[pl.ds(k, 1), :]
        low = col % width
        high = col // width
        hot = jnp.where(table_row == low.astype(jnp.int16), jnp.ones((), BF16), jnp.zeros((), BF16))
        hot_ref[k] = hot
        got = mm(table_ref[...], hot)
        first = got[0:dense]
        for block in range(1, blocks):
            first = jnp.where(high == block, got[block * dense : (block + 1) * dense], first)
        halves_ = []
        for part in range(own_tiles):
            lanes = slice(part * 128, (part + 1) * 128)
            within = jnp.broadcast_to((col % 128)[:, lanes], (8, 128))
            which = jnp.broadcast_to((col // 128)[:, lanes], (8, 128))
            found = [None] * (sparse // 8 + 1)
            for tile in range(all_tiles):
                here = which == tile
                for c in range(sparse // 8 + 1):
                    piece = lanes_ref[c * 8 : (c + 1) * 8, tile * 128 : (tile + 1) * 128]
                    piece = jnp.take_along_axis(piece, within, axis=1)
                    found[c] = piece if tile == 0 else jnp.where(here, piece, found[c])
            halves_.append(jnp.concatenate(found, axis=0))
        second = jnp.concatenate(halves_, axis=1)
        up = jnp.concatenate([first, second[0:sparse]], axis=0)
        upg_ref[k] = up.astype(BF16)
        rel = second[sparse : sparse + 8] - own_pos
        rel = rel + jnp.where(row8 == 0, shift_ref[pl.ds(k, 1), :], 0.0)
        dist = jnp.sqrt(jnp.sum(rel * rel, axis=0, keepdims=True) + 1.0)
        rel_ref[k] = jnp.where(row8 == 3, dist, rel)
        scaled = (dist - centres) * (1.0 / basis_width)
        basis = jnp.where(k < count, jnp.exp(-(scaled * scaled)), 0.0)
        bas_ref[k] = basis
        b_hi = basis.astype(BF16).astype(F32)
        b_lo = basis - b_hi
        stacked = jnp.concatenate([b_hi, b_lo, b_hi, jnp.zeros_like(b_hi)], axis=0).astype(BF16)
        msg_ref[k] = mm(rw3, stacked) * up
        return carry

    lax.fori_loop(0, slots, gather, 0, unroll=4)

    part = 16

    def gather_sums(block, carry):
        at = pl.ds(pl.multiple_of(block * part, part), part)
        sums = [jnp.zeros((part, atoms), F32) for _ in range(4)]
        for k in range(slots):
            message = msg_ref[k, at, :]
            sums[0] = sums[0] + message
            for axis in range(3):
                sums[axis + 1] = sums[axis + 1] + message * rel_ref[k, axis : axis + 1, :]
        for axis in range(4):
            sv_ref[axis, at, :] = sums[axis]
        return carry

    lax.fori_loop(0, channels // part, gather_sums, 0)

    scalar = sv_ref[0] * message_scale
    vectors = [sv_ref[axis + 1] * (message_scale * vector_scale) for axis in range(3)]
    invariant = scalar + scalar * scalar + (vectors[0] * vectors[0] + vectors[1] * vectors[1] + vectors[2] * vectors[2])
    w_out = w_out_ref[...]
    hidden = feat_ref[...].astype(F32) + mm(w_out, invariant.astype(BF16))
    square = iota((channels, channels), 0) == iota((channels, channels), 1)
    ew = jnp.sum(jnp.where(square, ew_ref[...].astype(F32), 0.0), axis=1, keepdims=True)
    gate = 1.0 / (1.0 + jnp.exp(-hidden))
    eshort_ref[...] = jnp.sum(ew * (hidden * gate), axis=0, keepdims=True)
    d_hidden = ew * (gate * (1.0 + hidden * (1.0 - gate)))
    dh_hi, dh_lo = split2(d_hidden)
    d_inv = (mm_tn(w_out, dh_hi) + mm_tn(w_out, dh_lo)).astype(BF16).astype(F32)
    sv_ref[0] = d_inv * (1.0 + 2.0 * scalar) * message_scale
    for axis in range(3):
        sv_ref[axis + 1] = d_inv * vectors[axis] * (2.0 * message_scale * vector_scale)

    acc_ref[...] = jnp.zeros_like(acc_ref)
    reduce_left = jnp.concatenate([rwt_hi.astype(F32), rwt_lo.astype(F32)], axis=0).astype(BF16)
    chunk = 32

    def scatter(k, total):
        rel8 = rel_ref[k]
        basis = bas_ref[k]
        dist = rel8[3:4]
        turns = [jnp.zeros((8, atoms), F32) for _ in range(3)]
        right = []
        for first in range(0, channels, chunk):
            at = slice(first, first + chunk)
            message = msg_ref[k, at, :]
            pull = sv_ref[0, at, :]
            for axis in range(3):
                side = sv_ref[axis + 1, at, :]
                pull = pull + side * rel8[axis : axis + 1]
                turn = side * message
                for r in range(0, chunk, 8):
                    turns[axis] = turns[axis] + turn[r : r + 8]
            right.append((pull * upg_ref[k, at, :].astype(F32)).astype(BF16))
        sums = mm(reduce_left, jnp.concatenate(right, axis=0))
        d_basis = sums[0:8] + sums[8:16]
        slope = d_basis * basis * ((dist - centres) * (-2.0 / (basis_width * basis_width)))
        d_dist = jnp.sum(slope, axis=0, keepdims=True) / dist
        d_rel = jnp.where(row8 < 3, d_dist * rel8, 0.0)
        for axis in range(3):
            d_rel = d_rel + jnp.where(row8 == axis, jnp.sum(turns[axis], axis=0, keepdims=True), 0.0)
        d_hi = d_rel.astype(BF16).astype(F32)
        both = d_hi + pltpu.roll(d_rel - d_hi, 4, 0)
        high = col_ref[pl.ds(k, 1), :] // width
        left = jnp.concatenate([jnp.where(high == block, both, 0.0) for block in range(blocks)], axis=0)
        acc_ref[...] += mm_nt(left.astype(BF16), hot_ref[k])
        return total + d_rel

    total = lax.fori_loop(0, slots, scatter, jnp.zeros((8, atoms), F32), unroll=4)

    def grad_tile(tile):
        block, piece = divmod(tile, tiles)
        g = acc_ref[block * 8 : block * 8 + 8, piece * 128 : (piece + 1) * 128]
        return g + pltpu.roll(g, 4, 0)

    for tile in range(own_tiles):
        gown_ref[:, tile * 128 : (tile + 1) * 128] = grad_tile(tile) - total[:, tile * 128 : (tile + 1) * 128]

    send_ref[...] = jnp.zeros_like(send_ref)
    left1 = iota((1, 128), 1) < exported
    for u in range(all_tiles - own_tiles):
        g = grad_tile(own_tiles + u)
        swapped = pltpu.roll(g, 64, 1)
        for side in range(2):
            if 2 * u + side >= len(domains):
                continue
            a, b, c = domains[2 * u + side]
            device = lax.rem(places[0] + (a + counts[0]), counts[0]) * counts[1]
            device = (device + lax.rem(places[1] + (b + counts[1]), counts[1])) * counts[2]
            device = device + lax.rem(places[2] + (c + counts[2]), counts[2])
            here, there = (g, swapped) if side == 0 else (swapped, g)
            top = jnp.where(left1, here[0:1], there[1:2])
            bottom = jnp.where(left1, here[2:3], 0.0)
            send_ref[device, :, 0:128] += top
            send_ref[device, :, 128:256] += bottom


def spline(distance):
    outer = jnp.maximum(2.0 - distance, 0.0)
    inner = jnp.maximum(1.0 - distance, 0.0)
    return outer * outer * outer * (1.0 / 6.0) - inner * inner * inner * (4.0 / 6.0)


def weights_of(count, position):
    gap = (iota((count, position.shape[1]), 0) - 1).astype(F32) - position
    return spline(jnp.abs(gap))


def slopes_of(count, position):
    gap = (iota((count, position.shape[1]), 0) - 1).astype(F32) - position
    distance = jnp.abs(gap)
    outer = jnp.maximum(2.0 - distance, 0.0)
    inner = jnp.maximum(1.0 - distance, 0.0)
    size = outer * outer * 0.5 - inner * inner * 2.0
    return jnp.where(gap > 0.0, size, -size)


def spread_kernel(counts, groups, info_ref, *refs):
    count_x, count_y, count_z = counts
    rho_ref, plane_ref = refs[-2:]
    atoms = info_ref.shape[2] // 4
    tall = CY * count_y + 8
    rho_ref[...] = refs[0][...] if len(refs) > 2 else jnp.zeros_like(rho_ref)
    plane_ref[...] = jnp.zeros_like(plane_ref)

    def domain(number, slot):
        info = info_ref[number]
        wx = weights_of(16, info[:, 0:atoms]) * info[:, 3 * atoms : 4 * atoms]
        even = weights_of(24, info[:, atoms : 2 * atoms])
        odd = pltpu.roll(even, 4, 0)
        for x in range(0, XL, 2):
            first = x * YW
            here = wx[x : x + 1]
            plane_ref[slot, first : first + 16] = here * even[0:16]
            if x + 1 == XL:
                plane_ref[slot, first + 16 : first + 24] = here * even[16:24]
                continue
            there = wx[x + 1 : x + 2]
            plane_ref[slot, first + 16 : first + 24] = here * even[16:24] + there * odd[0:8]
            plane_ref[slot, first + 24 : first + 40] = there * odd[8:24]
        high, low = split2(weights_of(ZL, info[:, 2 * atoms : 3 * atoms]))
        plane_high, plane_low = split2(plane_ref[slot])
        both = mm_nt(jnp.concatenate([high, low], axis=0), plane_high)
        return both[0:ZL] + both[ZL : 2 * ZL] + mm_nt(high, plane_low)

    def spread(group, carry):
        grown = [domain(group * count_z + l, l % plane_ref.shape[0]) for l in range(count_z)]
        pieces = []
        for l in range(count_z):
            pieces.append(grown[l][0 : ZL - CZ] + grown[l - 1][CZ:ZL])
            pieces.append(grown[l][ZL - CZ : CZ])
        turned = jnp.transpose(jnp.concatenate(pieces, axis=0))
        first = (group // count_y * CX) * tall + (group % count_y) * CY
        for x in range(XL):
            at = pl.ds(pl.multiple_of(first + x * tall, 8), YW)
            rho_ref[at, :] += turned[x * YW : (x + 1) * YW]
        return carry

    lax.fori_loop(groups[0], groups[1], spread, 0)


def long_kernel(
    counts,
    grown_ref,
    pq_ref,
    hy_ref,
    hzh_ref,
    hzl_ref,
    kx_ref,
    kxo_ref,
    hyo_ref,
    hzoh_ref,
    hzol_ref,
    influence_ref,
    out_ref,
    rho_ref,
    spec_ref,
    back_ref,
    phi_ref,
):
    count_x, count_y, count_z = counts
    grid_x, grid_y, grid_z = CX * count_x, CY * count_y, CZ * count_z
    atoms = pq_ref.shape[1]
    tall = grid_y + 8
    rho_ref[...] = grown_ref[0 : grid_x * tall]
    place_x, place_y, place_z = [lax.axis_index(axis) for axis in MESH_AXES]
    for x in range(3):
        rho_ref[x * tall : (x + 1) * tall] += grown_ref[(grid_x + x) * tall : (grid_x + x + 1) * tall]

    def times_z(values, table_high, table_low):
        high, low = split2(values)
        return mm(high, table_high) + mm(high, table_low) + mm(low, table_high)

    def along_yz(x, carry):
        start = pl.multiple_of(x * tall, 8)
        top = rho_ref[pl.ds(start, 8), :] + rho_ref[pl.ds(start + grid_y, 8), :]
        values = jnp.concatenate([top, rho_ref[pl.ds(start + 8, grid_y - 8), :]], axis=0)
        turned = mm(hy_ref[...], stack3(values))
        spec_ref[pl.ds(pl.multiple_of(x * grid_y, 8), grid_y), :] = times_z(turned, hzh_ref[...], hzl_ref[...])
        return carry

    lax.fori_loop(0, grid_x, along_yz, 0, unroll=4)

    def along_x(octet, carry):
        def part(ref, x):
            return ref[pl.ds(pl.multiple_of(x * grid_y + octet * 8, 8), 8), :]

        values = jnp.concatenate([part(spec_ref, x) for x in range(grid_x)], axis=0)
        factor = jnp.concatenate([part(influence_ref, x) for x in range(grid_x)], axis=0)
        back = mm(kxo_ref[place_x], stack3(mm(kx_ref[...], stack3(values)) * factor))
        for x in range(XL):
            back_ref[pl.ds(pl.multiple_of(x * grid_y + octet * 8, 8), 8), :] = back[x * 8 : (x + 1) * 8]
        return carry

    lax.fori_loop(0, grid_y // 8, along_x, 0, unroll=2)

    for x in range(XL):
        turned = mm(hyo_ref[place_y], stack3(back_ref[x * grid_y : (x + 1) * grid_y]))
        phi_ref[x * YL : (x + 1) * YL] = times_z(turned, hzoh_ref[place_z], hzol_ref[place_z])[0:YL]

    own = pq_ref[...]
    charge = own[3:4]
    wx, dx = weights_of(16, own[0:1]), slopes_of(16, own[0:1])
    wy, dy = weights_of(YL, own[1:2]), slopes_of(YL, own[1:2])
    wzh, wzl = split2(jnp.concatenate([weights_of(128, own[2:3]), slopes_of(128, own[2:3])], axis=1))
    high, low = split2(phi_ref[...])
    lines = mm(high, wzh) + mm(high, wzl) + mm(low, wzh)
    potential = jnp.zeros((1, atoms), F32)
    field = [jnp.zeros((1, atoms), F32) for _ in range(3)]
    for x in range(XL):
        flat = lines[x * YL : (x + 1) * YL, 0:atoms]
        steep = lines[x * YL : (x + 1) * YL, atoms : 2 * atoms]
        s0 = jnp.sum(wy * flat, axis=0, keepdims=True)
        sy = jnp.sum(dy * flat, axis=0, keepdims=True)
        sz = jnp.sum(wy * steep, axis=0, keepdims=True)
        here = wx[x : x + 1]
        potential = potential + here * s0
        field[0] = field[0] + dx[x : x + 1] * s0
        field[1] = field[1] + here * sy
        field[2] = field[2] + here * sz
    out_ref[...] = jnp.zeros_like(out_ref)
    for axis in range(3):
        out_ref[axis : axis + 1] = charge * field[axis]
    out_ref[3:4] = 0.5 * charge * potential


def final_kernel(recv_ref, gown_ref, eshort_ref, long_ref, export_ref, forces_ref, energy_ref):
    atoms = gown_ref.shape[1]

    def returned(device, sums):
        return sums + recv_ref[device]

    sums = lax.fori_loop(0, recv_ref.shape[0], returned, jnp.zeros((1, 256), F32), unroll=8)
    energy_ref[...] = eshort_ref[...] + long_ref[3:4]
    row8 = iota((8, 128), 0)
    lines3 = (sums[:, 0:128], pltpu.roll(jnp.broadcast_to(sums[:, 0:128], (8, 128)), 64, 1), sums[:, 128:256])
    lent = jnp.zeros((8, 128), F32)
    for axis in range(3):
        lent = jnp.where(row8 == axis, lines3[axis], lent)
    lent = jnp.where(iota((8, 128), 1) < 64, lent, 0.0)
    export = export_ref[...]
    twice = jnp.concatenate([export, export], axis=1)
    hot = jnp.where(iota((atoms, 128), 0) == twice, 1.0, 0.0).astype(BF16)
    high, low = split2(lent)
    rest = (lent - high.astype(F32) - low.astype(F32)).astype(BF16)
    back = mm_nt(high, hot) + mm_nt(low, hot) + mm_nt(rest, hot)
    for axis in range(3):
        total = long_ref[axis : axis + 1] + gown_ref[axis : axis + 1] + back[axis : axis + 1]
        forces_ref[axis : axis + 1] = -total


def cas_table(extent):
    indices = np.arange(extent)
    angle = (indices[:, None] * indices[None, :] % extent) * (2.0 * np.pi / extent)
    return (np.cos(angle) + np.sin(angle)) / np.sqrt(extent)


def halves(table):
    high = np.asarray(table, np.float32).astype(BF16)
    low = (np.asarray(table, np.float64) - high.astype(np.float64)).astype(np.float32).astype(BF16)
    return high, low


def wide(table):
    high, low = halves(table)
    return np.concatenate([high, high, low], axis=-1)


def wave_squares(extent):
    folded = (np.arange(extent) + extent // 2) % extent - extent // 2
    return (folded * (2.0 * np.pi / extent)) ** 2


def exchange(block, axis):
    size = lax.axis_size(axis)
    up = [(i, (i + 1) % size) for i in range(size)]
    if size <= 2:
        other = lax.ppermute(block, axis, up)
        return other, other
    return lax.ppermute(block, axis, up), lax.ppermute(block, axis, [(j, i) for i, j in up])


def per_device(
    atom_cell,
    atom_frac,
    features,
    ghost_export,
    neighbors,
    neighbor_count,
    w_up,
    radial_weight,
    w_out,
    energy_weight,
    charge_weight,
):
    channels, atoms = features.shape
    exported = ghost_export.shape[0]
    slots = neighbors.shape[1]
    counts = tuple(lax.axis_size(axis) for axis in MESH_AXES)
    count_x, count_y, count_z = counts
    devices = count_x * count_y * count_z
    half = channels // 2
    rows = channels + 16

    record, own, pq, info = pl.pallas_call(
        prep_kernel,
        out_shape=(
            jax.ShapeDtypeStruct((half + 16, 2 * exported), BF16),
            jax.ShapeDtypeStruct((rows, atoms), BF16),
            jax.ShapeDtypeStruct((8, atoms), F32),
            jax.ShapeDtypeStruct((devices, 1, 4 * atoms), F32),
        ),
        in_specs=[VMEM] * 6,
        out_specs=(VMEM,) * 4,
        scratch_shapes=[pltpu.VMEM((16, atoms), F32)],
        name="prep",
    )(features, atom_cell, atom_frac, ghost_export[None, :], w_up, charge_weight[None, :])

    info = lax.all_to_all(info, ("gx", "gy", "gz"), split_axis=0, concat_axis=0, tiled=True)
    grid_x, grid_y, grid_z = CX * count_x, CY * count_y, CZ * count_z
    grown_shape = ((grid_x + 3) * (grid_y + 8), grid_z)

    def spread(groups, *arrays):
        return pl.pallas_call(
            functools.partial(spread_kernel, counts, groups),
            out_shape=jax.ShapeDtypeStruct(grown_shape, F32),
            in_specs=[VMEM] * len(arrays),
            out_specs=VMEM,
            scratch_shapes=[pltpu.VMEM((count_z, 256, atoms), F32)],
            compiler_params=PARAMS,
            name="spread",
        )(*arrays)

    columns = count_x * count_y
    block = record[None]
    below, above = exchange(block, "gx")
    if count_x <= 2:
        block = jnp.concatenate([block, below], axis=0)
        x_of = (1, 0, 1)
    else:
        block = jnp.concatenate([below, block, above], axis=0)
        x_of = (0, 1, 2)
    below, above = exchange(block, "gy")
    grown = spread((0, columns // 2), info)
    below, above, grown = lax.optimization_barrier((below, above, grown))
    block = jnp.concatenate([below, block, above], axis=0)
    below, above = exchange(block, "gz")
    grown = spread((columns // 2, columns), info, grown)
    below, above, grown = lax.optimization_barrier((below, above, grown))

    domains = lent_domains(count_x)
    width = 256
    dense = 80
    all_tiles = -(-(atoms + len(domains) * exported) // 128)
    blocks = -(-all_tiles * 128 // width)
    send, gown, eshort = pl.pallas_call(
        functools.partial(short_kernel, (counts, x_of, exported, dense)),
        out_shape=(
            jax.ShapeDtypeStruct((devices, 1, 256), F32),
            jax.ShapeDtypeStruct((8, atoms), F32),
            jax.ShapeDtypeStruct((1, atoms), F32),
        ),
        in_specs=[VMEM] * 11,
        out_specs=(VMEM,) * 3,
        scratch_shapes=[
            pltpu.VMEM((blocks * dense, width), BF16),
            pltpu.VMEM((channels - dense + 8, all_tiles * 128), F32),
            pltpu.VMEM((slots, width, atoms), BF16),
            pltpu.VMEM((slots, channels, atoms), BF16),
            pltpu.VMEM((slots, channels, atoms), F32),
            pltpu.VMEM((slots, 8, atoms), F32),
            pltpu.VMEM((slots, 8, atoms), F32),
            pltpu.VMEM((4, channels, atoms), F32),
            pltpu.VMEM((slots, atoms), F32),
            pltpu.VMEM((slots, atoms), jnp.int32),
            pltpu.VMEM((blocks * 8, width), F32),
        ],
        compiler_params=PARAMS,
        name="short",
    )(
        below,
        block,
        above,
        own,
        neighbors.T,
        neighbor_count[None, :],
        pq,
        features,
        radial_weight.T,
        w_out,
        energy_weight[None, :],
    )

    recv = lax.all_to_all(send, ("gx", "gy", "gz"), split_axis=0, concat_axis=0, tiled=True)

    cas_x, cas_y, cas_z = cas_table(grid_x), cas_table(grid_y), cas_table(grid_z)
    square = (
        wave_squares(grid_x)[:, None, None] + wave_squares(grid_y)[None, :, None] + wave_squares(grid_z)[None, None, :]
    )
    safe = np.where(square > 0.0, square, 1.0)
    influence = np.where(square > 0.0, 4.0 * math.pi * np.exp(-square / (4.0 * ewald_beta_sq)) / safe, 0.0)
    influence = influence.reshape(grid_x * grid_y, grid_z).astype(np.float32)
    eye = np.eye(8)
    kx = wide(np.kron(cas_x, eye))
    x_rows = (np.arange(count_x)[:, None] * CX + np.arange(XL + 1)[None, :]) % grid_x
    kxo = np.stack([wide(np.kron(cas_x[r], eye)) for r in x_rows])
    y_rows = (np.arange(count_y)[:, None] * CY + np.arange(32)[None, :]) % grid_y
    hyo = np.stack([wide(cas_y[r]) for r in y_rows])
    z_rows = (np.arange(count_z)[:, None] * CZ + np.arange(128)[None, :]) % grid_z
    hzo = [halves(cas_z[:, r] * (np.arange(128) < ZL)[None, :]) for r in z_rows]
    hzoh, hzol = np.stack([t[0] for t in hzo]), np.stack([t[1] for t in hzo])
    hzh, hzl = halves(cas_z)

    far = pl.pallas_call(
        functools.partial(long_kernel, counts),
        out_shape=jax.ShapeDtypeStruct((8, atoms), F32),
        in_specs=[VMEM] * 11,
        out_specs=VMEM,
        cost_estimate=pl.CostEstimate(flops=8_000_000_000, transcendentals=0, bytes_accessed=2_000_000),
        scratch_shapes=[
            pltpu.VMEM((grid_x * (grid_y + 8), grid_z), F32),
            pltpu.VMEM((grid_x * grid_y, grid_z), F32),
            pltpu.VMEM((XL * grid_y, grid_z), F32),
            pltpu.VMEM((XL * YL, 128), F32),
        ],
        compiler_params=PARAMS,
        name="long",
    )(
        grown,
        pq,
        jnp.asarray(wide(cas_y)),
        jnp.asarray(hzh),
        jnp.asarray(hzl),
        jnp.asarray(kx),
        jnp.asarray(kxo),
        jnp.asarray(hyo),
        jnp.asarray(hzoh),
        jnp.asarray(hzol),
        jnp.asarray(influence),
    )
    forces, energy = pl.pallas_call(
        final_kernel,
        out_shape=(jax.ShapeDtypeStruct((3, atoms), F32), jax.ShapeDtypeStruct((1, atoms), F32)),
        in_specs=[VMEM] * 5,
        out_specs=(VMEM,) * 2,
        name="final",
    )(recv, gown, eshort, far, ghost_export[None, :])
    return (forces, energy.reshape(-1))


def solution(mesh):
    spread = ("gx", "gy", "gz")
    in_specs = (
        P(None, spread),
        P(None, spread),
        P(None, spread),
        P(spread),
        P(spread, None),
        P(spread),
        P(),
        P(),
        P(),
        P(),
        P(),
    )
    out_specs = (P(None, spread), P(spread))
    return jax.shard_map(per_device, mesh=mesh, in_specs=in_specs, out_specs=out_specs, check_vma=False)
```

```python
import functools
import math

import jax
import jax.numpy as jnp
import numpy as np
from jax import lax
from jax.experimental import pallas as pl
from jax.experimental.pallas import tpu as pltpu
from jax.sharding import PartitionSpec as P

CX = 8
CY = 16
CZ = 64
XL = CX + 3
YL = CY + 8
YW = CY + 4
ZL = CZ + 16

basis_step = 1.4
basis_width = 1.4
message_scale = 0.125
vector_scale = 1.0 / 6.0
ewald_beta_sq = 2.0

F32 = jnp.float32
BF16 = jnp.bfloat16
VMEM = pl.BlockSpec(memory_space=pltpu.VMEM)
MESH_AXES = ("gx", "gy", "gz")
PARAMS = pltpu.CompilerParams(vmem_limit_bytes=24 * 1024 * 1024)


def iota(shape, dim):
    return lax.broadcasted_iota(jnp.int32, shape, dim)


def mm(a, b):
    return jnp.dot(a, b, preferred_element_type=F32)


def mm_nt(a, b):
    return lax.dot_general(a, b, (((1,), (1,)), ((), ())), preferred_element_type=F32)


def mm_tn(a, b):
    return lax.dot_general(a, b, (((0,), (0,)), ((), ())), preferred_element_type=F32)


def split2(values):
    high = values.astype(BF16)
    return high, (values - high.astype(F32)).astype(BF16)


def stack3(values):
    high, low = split2(values)
    return jnp.concatenate([high, low, high], axis=0)


def prep_kernel(feat_ref, cell_ref, frac_ref, export_ref, w_up_ref, cw_ref, rec_ref, own_ref, pq_ref, info_ref, p16_ref):
    channels, atoms = feat_ref.shape
    half = channels // 2
    exported = export_ref.shape[1]
    feat = feat_ref[...]
    up = mm(w_up_ref[...], feat).astype(BF16)
    charge = mm(jnp.broadcast_to(cw_ref[...], (16, channels)), feat)[0:1]
    cell = cell_ref[...].astype(F32)
    frac = frac_ref[...].astype(F32)
    p16_ref[...] = jnp.zeros_like(p16_ref)
    p16_ref[0:3] = cell
    p16_ref[8:11] = frac
    pq_ref[...] = jnp.zeros_like(pq_ref)
    pq_ref[0:3] = cell + frac
    pq_ref[3:4] = charge
    p16 = p16_ref[...].astype(BF16)
    own_ref[0:channels] = up
    own_ref[channels : channels + 16] = p16
    export = export_ref[...]
    twice = jnp.concatenate([export, export], axis=1)
    pick = jnp.where(iota((atoms, 2 * exported), 0) == twice, 1.0, 0.0).astype(BF16)
    first = mm(up[0:half], pick)
    second = mm(up[half:channels], pick)
    left = iota((half, 2 * exported), 1) < exported
    rec_ref[0:half] = jnp.where(left, first, second).astype(BF16)
    rec_ref[half : half + 16] = mm(p16, pick).astype(BF16)
    info = [pq_ref[r : r + 1, :] for r in range(4)]

    def fill(device, carry):
        for r in range(4):
            info_ref[device, :, r * atoms : (r + 1) * atoms] = info[r]
        return carry

    lax.fori_loop(0, info_ref.shape[0], fill, 0, unroll=8)


def lent_domains(count_x):
    around = [(b, c) for b in (-1, 0, 1) for c in (-1, 0, 1)]
    if count_x <= 2:
        return [(0, b, c) for b, c in around if (b, c) != (0, 0)] + [(1, b, c) for b, c in around]
    return [(a, b, c) for a in (-1, 0, 1) for b, c in around if (a, b, c) != (0, 0, 0)]


def short_kernel(
    setup,
    before_ref,
    mid_ref,
    after_ref,
    own_ref,
    nbr_ref,
    count_ref,
    pq_ref,
    feat_ref,
    rwt_ref,
    w_out_ref,
    ew_ref,
    send_ref,
    gown_ref,
    eshort_ref,
    table_ref,
    lanes_ref,
    hot_ref,
    upg_ref,
    msg_ref,
    rel_ref,
    bas_ref,
    sv_ref,
    svb_ref,
    shift_ref,
    col_ref,
    acc_ref,
):
    counts, x_of, exported, dense = setup
    count_x = counts[0]
    places = [lax.axis_index(axis) for axis in MESH_AXES]
    channels, atoms = feat_ref.shape
    half = channels // 2
    slots = nbr_ref.shape[0]
    width = table_ref.shape[1]
    blocks = table_ref.shape[0] // dense
    tiles = width // 128
    own_tiles = atoms // 128
    sparse = channels - dense
    all_tiles = lanes_ref.shape[1] // 128
    arrays = (before_ref, mid_ref, after_ref)
    per_axis = mid_ref.shape[0] // 3
    domains = lent_domains(count_x)

    def put(tile, up, pos):
        block, part = divmod(tile, tiles)
        lanes = slice(part * 128, (part + 1) * 128)
        for group in range(dense // 16):
            first = (group * blocks + block) * 16
            table_ref[first : first + 16, lanes] = up[group * 16 : group * 16 + 16].astype(BF16)
        lanes = slice(tile * 128, (tile + 1) * 128)
        if sparse:
            lanes_ref[0:sparse, lanes] = up[dense:channels]
        lanes_ref[sparse : sparse + 8, lanes] = pos

    last = blocks * tiles
    for tile in range(all_tiles, last):
        block, part = divmod(tile, tiles)
        for group in range(dense // 16):
            first = (group * blocks + block) * 16
            table_ref[first : first + 16, part * 128 : (part + 1) * 128] = jnp.zeros((16, 128), BF16)
    for tile in range(own_tiles):
        lanes = slice(tile * 128, (tile + 1) * 128)
        both = own_ref[:, lanes].astype(F32)
        put(tile, both[0:channels], both[channels : channels + 8] + both[channels + 8 : channels + 16])
    left64 = iota((half, 128), 1) < exported
    left16 = iota((16, 128), 1) < exported
    left8 = iota((8, 128), 1) < exported
    row8 = iota((8, 128), 0)
    for u in range(all_tiles - own_tiles):
        even = domains[2 * u]
        odd = domains[2 * u + 1] if 2 * u + 1 < len(domains) else None

        def record(domain):
            return arrays[domain[2] + 1][(domain[1] + 1) * per_axis + x_of[domain[0] + 1]].astype(F32)

        e = record(even)
        o = record(odd) if odd else jnp.zeros_like(e)
        odd = odd or (0, 0, 0)
        low = jnp.where(left64, e[0:half], pltpu.roll(o[0:half], 64, 1))
        high = jnp.where(left64, pltpu.roll(e[0:half], 64, 1), o[0:half])
        pos = jnp.where(left16, e[half : half + 16], o[half : half + 16])
        pos = pos[0:8] + pos[8:16]
        for axis, extent in ((1, CY), (2, CZ)):
            shift = jnp.where(left8, float(even[axis] * extent), float(odd[axis] * extent))
            pos = pos + jnp.where(row8 == axis, shift, 0.0)
        put(own_tiles + u, jnp.concatenate([low, high], axis=0), pos)

    index = nbr_ref[...]
    rank = index - atoms
    row = 9 * exported
    if count_x <= 2:
        inner = rank - row
        inner = jnp.where(inner >= 5 * exported, inner - exported, inner)
        outer = jnp.where(rank < row, rank, rank - 2 * row) + 8 * exported
        place = jnp.where(jnp.logical_and(rank >= row, rank < 2 * row), inner, outer)
    else:
        place = jnp.where(rank >= 14 * exported, rank - exported, rank)
    col_ref[...] = jnp.where(rank < 0, index, place + atoms)
    ahead = jnp.where(rank < row, -float(CX), jnp.where(rank < 2 * row, 0.0, float(CX)))
    shift_ref[...] = jnp.where(rank < 0, 0.0, ahead)

    row8 = iota((8, atoms), 0)
    own_pos = jnp.where(row8 < 3, pq_ref[...], 0.0)
    count = count_ref[...]
    centres = iota((8, atoms), 0).astype(F32) * basis_step
    table_row = iota((width, atoms), 0).astype(jnp.int16)
    rwt = rwt_ref[...]
    rwt_hi, rwt_lo = split2(rwt)
    rw3 = jnp.concatenate([rwt_hi.astype(F32), rwt_hi.astype(F32), rwt_lo.astype(F32), jnp.zeros_like(rwt)], axis=0)
    rw3 = jnp.transpose(jnp.concatenate([rw3, jnp.zeros((96, channels), F32)], axis=0))[:, 0:32].astype(BF16)

    def gather(k):
        col = col_ref[pl.ds(k, 1), :]
        low = col % width
        high = col // width
        hot = jnp.where(table_row == low.astype(jnp.int16), jnp.ones((), BF16), jnp.zeros((), BF16))
        hot_ref[k] = hot
        got = mm(table_ref[...], hot)
        first = []
        for group in range(dense // 16):
            rows = [got[(group * blocks + block) * 16 : (group * blocks + block + 1) * 16] for block in range(blocks)]
            value = rows[0]
            for block in range(1, blocks):
                value = jnp.where(high == block, rows[block], value)
            first.append(value)
        halves_ = []
        for part in range(own_tiles):
            lanes = slice(part * 128, (part + 1) * 128)
            within = jnp.broadcast_to((col % 128)[:, lanes], (8, 128))
            which = jnp.broadcast_to((col // 128)[:, lanes], (8, 128))
            found = [None] * (sparse // 8 + 1)
            for tile in range(all_tiles):
                here = which == tile
                for c in range(sparse // 8 + 1):
                    piece = lanes_ref[c * 8 : (c + 1) * 8, tile * 128 : (tile + 1) * 128]
                    piece = jnp.take_along_axis(piece, within, axis=1)
                    found[c] = piece if tile == 0 else jnp.where(here, piece, found[c])
            halves_.append(jnp.concatenate(found, axis=0))
        second = jnp.concatenate(halves_, axis=1)
        up = jnp.concatenate(first + ([second[0:sparse]] if sparse else []), axis=0)
        upg_ref[k] = up.astype(BF16)
        rel = second[sparse : sparse + 8] - own_pos
        rel = rel + jnp.where(row8 == 0, shift_ref[pl.ds(k, 1), :], 0.0)
        dist = jnp.sqrt(jnp.sum(rel * rel, axis=0, keepdims=True) + 1.0)
        rel_ref[k] = jnp.where(row8 == 3, dist, rel)
        scaled = (dist - centres) * (1.0 / basis_width)
        basis = jnp.where(k < count, jnp.exp(-(scaled * scaled)), 0.0)
        bas_ref[k] = basis
        b_hi = basis.astype(BF16).astype(F32)
        b_lo = basis - b_hi
        stacked = jnp.concatenate([b_hi, b_lo, b_hi, jnp.zeros_like(b_hi)], axis=0).astype(BF16)
        message = mm(rw3, stacked) * up
        msg_ref[k] = message
        return message, rel

    part = 16
    stride = math.gcd(slots, 8)
    sv_ref[...] = jnp.zeros_like(sv_ref)

    def gather_some(number, carry):
        found = [gather(number * stride + step) for step in range(stride)]
        for first in range(0, channels, part):
            sums = [sv_ref[axis, first : first + part] for axis in range(4)]
            for step in range(stride):
                message = msg_ref[number * stride + step, first : first + part]
                rel = found[step][1]
                sums[0] = sums[0] + message
                for axis in range(3):
                    sums[axis + 1] = sums[axis + 1] + message * rel[axis : axis + 1]
            for axis in range(4):
                sv_ref[axis, first : first + part] = sums[axis]
        return carry

    lax.fori_loop(0, slots // stride, gather_some, 0)

    scalar = sv_ref[0] * message_scale
    vectors = [sv_ref[axis + 1] * (message_scale * vector_scale) for axis in range(3)]
    invariant = scalar + scalar * scalar + (vectors[0] * vectors[0] + vectors[1] * vectors[1] + vectors[2] * vectors[2])
    w_out = w_out_ref[...]
    hidden = feat_ref[...].astype(F32) + mm(w_out, invariant.astype(BF16))
    square = iota((channels, channels), 0) == iota((channels, channels), 1)
    ew = jnp.sum(jnp.where(square, ew_ref[...].astype(F32), 0.0), axis=1, keepdims=True)
    gate = 1.0 / (1.0 + jnp.exp(-hidden))
    eshort_ref[...] = jnp.sum(ew * (hidden * gate), axis=0, keepdims=True)
    d_hidden = ew * (gate * (1.0 + hidden * (1.0 - gate)))
    dh_hi, dh_lo = split2(d_hidden)
    d_inv = (mm_tn(w_out, dh_hi) + mm_tn(w_out, dh_lo)).astype(BF16).astype(F32)
    for axis in range(4):
        factor = (1.0 + 2.0 * scalar) * message_scale if axis == 0 else vectors[axis - 1] * (2.0 * message_scale * vector_scale)
        sv_ref[axis] = d_inv * factor
        svb_ref[axis] = (d_inv * factor).astype(BF16)

    acc_ref[...] = jnp.zeros_like(acc_ref)
    reduce_left = jnp.concatenate([rwt_hi.astype(F32), rwt_lo.astype(F32)], axis=0).astype(BF16)
    chunk = 32

    def scatter(k, total):
        rel8 = rel_ref[k]
        basis = bas_ref[k]
        dist = rel8[3:4]
        rel_low = [rel8[axis : axis + 1].astype(BF16) for axis in range(3)]
        turns = [jnp.zeros((8, atoms), F32) for _ in range(3)]
        right = []
        for first in range(0, channels, chunk):
            at = slice(first, first + chunk)
            message = msg_ref[k, at, :]
            pull = svb_ref[0, at, :]
            for axis in range(3):
                pull = pull + svb_ref[axis + 1, at, :] * rel_low[axis]
                turn = sv_ref[axis + 1, at, :] * message
                for r in range(0, chunk, 8):
                    turns[axis] = turns[axis] + turn[r : r + 8]
            right.append(pull * upg_ref[k, at, :])
        sums = mm(reduce_left, jnp.concatenate(right, axis=0))
        d_basis = sums[0:8] + sums[8:16]
        slope = d_basis * basis * ((dist - centres) * (-2.0 / (basis_width * basis_width)))
        d_dist = jnp.sum(slope, axis=0, keepdims=True) / dist
        d_rel = jnp.where(row8 < 3, d_dist * rel8, 0.0)
        for axis in range(3):
            d_rel = d_rel + jnp.where(row8 == axis, jnp.sum(turns[axis], axis=0, keepdims=True), 0.0)
        d_hi = d_rel.astype(BF16).astype(F32)
        both = d_hi + pltpu.roll(d_rel - d_hi, 4, 0)
        high = col_ref[pl.ds(k, 1), :] // width
        left = jnp.concatenate([jnp.where(high == block, both, 0.0) for block in range(blocks)], axis=0)
        acc_ref[...] += mm_nt(left.astype(BF16), hot_ref[k])
        return total + d_rel

    total = lax.fori_loop(0, slots, scatter, jnp.zeros((8, atoms), F32), unroll=4)

    def grad_tile(tile):
        block, piece = divmod(tile, tiles)
        g = acc_ref[block * 8 : block * 8 + 8, piece * 128 : (piece + 1) * 128]
        return g + pltpu.roll(g, 4, 0)

    for tile in range(own_tiles):
        gown_ref[:, tile * 128 : (tile + 1) * 128] = grad_tile(tile) - total[:, tile * 128 : (tile + 1) * 128]

    send_ref[...] = jnp.zeros_like(send_ref)
    left1 = iota((1, 128), 1) < exported
    for u in range(all_tiles - own_tiles):
        g = grad_tile(own_tiles + u)
        swapped = pltpu.roll(g, 64, 1)
        for side in range(2):
            if 2 * u + side >= len(domains):
                continue
            a, b, c = domains[2 * u + side]
            device = lax.rem(places[0] + (a + counts[0]), counts[0]) * counts[1]
            device = (device + lax.rem(places[1] + (b + counts[1]), counts[1])) * counts[2]
            device = device + lax.rem(places[2] + (c + counts[2]), counts[2])
            here, there = (g, swapped) if side == 0 else (swapped, g)
            top = jnp.where(left1, here[0:1], there[1:2])
            bottom = jnp.where(left1, here[2:3], 0.0)
            send_ref[device, :, 0:128] += top
            send_ref[device, :, 128:256] += bottom


def spline(distance):
    outer = jnp.maximum(2.0 - distance, 0.0)
    inner = jnp.maximum(1.0 - distance, 0.0)
    return outer * outer * outer * (1.0 / 6.0) - inner * inner * inner * (4.0 / 6.0)


def weights_of(count, position):
    gap = (iota((count, position.shape[1]), 0) - 1).astype(F32) - position
    return spline(jnp.abs(gap))


def slopes_of(count, position):
    gap = (iota((count, position.shape[1]), 0) - 1).astype(F32) - position
    distance = jnp.abs(gap)
    outer = jnp.maximum(2.0 - distance, 0.0)
    inner = jnp.maximum(1.0 - distance, 0.0)
    size = outer * outer * 0.5 - inner * inner * 2.0
    return jnp.where(gap > 0.0, size, -size)


def spread_kernel(counts, groups, info_ref, *refs):
    count_x, count_y, count_z = counts
    rho_ref, plane_ref = refs[-2:]
    atoms = info_ref.shape[2] // 4
    tall = CY * count_y + 8
    rho_ref[...] = refs[0][...] if len(refs) > 2 else jnp.zeros_like(rho_ref)
    plane_ref[...] = jnp.zeros_like(plane_ref)

    def domain(number, slot):
        info = info_ref[number]
        wx = weights_of(16, info[:, 0:atoms]) * info[:, 3 * atoms : 4 * atoms]
        even = weights_of(24, info[:, atoms : 2 * atoms])
        odd = pltpu.roll(even, 4, 0)
        for x in range(0, XL, 2):
            first = x * YW
            here = wx[x : x + 1]
            plane_ref[slot, first : first + 16] = here * even[0:16]
            if x + 1 == XL:
                plane_ref[slot, first + 16 : first + 24] = here * even[16:24]
                continue
            there = wx[x + 1 : x + 2]
            plane_ref[slot, first + 16 : first + 24] = here * even[16:24] + there * odd[0:8]
            plane_ref[slot, first + 24 : first + 40] = there * odd[8:24]
        high, low = split2(weights_of(ZL, info[:, 2 * atoms : 3 * atoms]))
        plane_high, plane_low = split2(plane_ref[slot])
        both = mm_nt(jnp.concatenate([high, low], axis=0), plane_high)
        return both[0:ZL] + both[ZL : 2 * ZL] + mm_nt(high, plane_low)

    def spread(group, carry):
        grown = [domain(group * count_z + l, l % plane_ref.shape[0]) for l in range(count_z)]
        pieces = []
        for l in range(count_z):
            pieces.append(grown[l][0 : ZL - CZ] + grown[l - 1][CZ:ZL])
            pieces.append(grown[l][ZL - CZ : CZ])
        turned = jnp.transpose(jnp.concatenate(pieces, axis=0))
        first = (group // count_y * CX) * tall + (group % count_y) * CY
        for x in range(XL):
            at = pl.ds(pl.multiple_of(first + x * tall, 8), YW)
            rho_ref[at, :] += turned[x * YW : (x + 1) * YW]
        return carry

    lax.fori_loop(groups[0], groups[1], spread, 0)


def long_kernel(
    counts,
    grown_ref,
    pq_ref,
    hy_ref,
    hzh_ref,
    hzl_ref,
    kx_ref,
    kxo_ref,
    hyo_ref,
    hzoh_ref,
    hzol_ref,
    influence_ref,
    out_ref,
    rho_ref,
    spec_ref,
    back_ref,
    phi_ref,
):
    count_x, count_y, count_z = counts
    grid_x, grid_y, grid_z = CX * count_x, CY * count_y, CZ * count_z
    atoms = pq_ref.shape[1]
    tall = grid_y + 8
    rho_ref[...] = grown_ref[0 : grid_x * tall]
    place_x, place_y, place_z = [lax.axis_index(axis) for axis in MESH_AXES]
    for x in range(3):
        rho_ref[x * tall : (x + 1) * tall] += grown_ref[(grid_x + x) * tall : (grid_x + x + 1) * tall]

    def times_z(values, table_high, table_low):
        high, low = split2(values)
        return mm(high, table_high) + mm(high, table_low) + mm(low, table_high)

    def along_yz(x, carry):
        start = pl.multiple_of(x * tall, 8)
        top = rho_ref[pl.ds(start, 8), :] + rho_ref[pl.ds(start + grid_y, 8), :]
        values = jnp.concatenate([top, rho_ref[pl.ds(start + 8, grid_y - 8), :]], axis=0)
        turned = mm(hy_ref[...], stack3(values))
        spec_ref[pl.ds(pl.multiple_of(x * grid_y, 8), grid_y), :] = times_z(turned, hzh_ref[...], hzl_ref[...])
        return carry

    lax.fori_loop(0, grid_x, along_yz, 0, unroll=4)

    def along_x(octet, carry):
        def part(ref, x):
            return ref[pl.ds(pl.multiple_of(x * grid_y + octet * 8, 8), 8), :]

        values = jnp.concatenate([part(spec_ref, x) for x in range(grid_x)], axis=0)
        factor = jnp.concatenate([part(influence_ref, x) for x in range(grid_x)], axis=0)
        back = mm(kxo_ref[place_x], stack3(mm(kx_ref[...], stack3(values)) * factor))
        for x in range(XL):
            back_ref[pl.ds(pl.multiple_of(x * grid_y + octet * 8, 8), 8), :] = back[x * 8 : (x + 1) * 8]
        return carry

    lax.fori_loop(0, grid_y // 8, along_x, 0, unroll=2)

    for x in range(XL):
        turned = mm(hyo_ref[place_y], stack3(back_ref[x * grid_y : (x + 1) * grid_y]))
        phi_ref[x * YL : (x + 1) * YL] = times_z(turned, hzoh_ref[place_z], hzol_ref[place_z])[0:YL]

    own = pq_ref[...]
    charge = own[3:4]
    wx, dx = weights_of(16, own[0:1]), slopes_of(16, own[0:1])
    wy, dy = weights_of(YL, own[1:2]), slopes_of(YL, own[1:2])
    wzh, wzl = split2(jnp.concatenate([weights_of(128, own[2:3]), slopes_of(128, own[2:3])], axis=1))
    high, low = split2(phi_ref[...])
    lines = mm(high, wzh) + mm(high, wzl) + mm(low, wzh)
    potential = jnp.zeros((1, atoms), F32)
    field = [jnp.zeros((1, atoms), F32) for _ in range(3)]
    for x in range(XL):
        flat = lines[x * YL : (x + 1) * YL, 0:atoms]
        steep = lines[x * YL : (x + 1) * YL, atoms : 2 * atoms]
        s0 = jnp.sum(wy * flat, axis=0, keepdims=True)
        sy = jnp.sum(dy * flat, axis=0, keepdims=True)
        sz = jnp.sum(wy * steep, axis=0, keepdims=True)
        here = wx[x : x + 1]
        potential = potential + here * s0
        field[0] = field[0] + dx[x : x + 1] * s0
        field[1] = field[1] + here * sy
        field[2] = field[2] + here * sz
    out_ref[...] = jnp.zeros_like(out_ref)
    for axis in range(3):
        out_ref[axis : axis + 1] = charge * field[axis]
    out_ref[3:4] = 0.5 * charge * potential


def final_kernel(recv_ref, gown_ref, eshort_ref, long_ref, export_ref, forces_ref, energy_ref):
    atoms = gown_ref.shape[1]

    def returned(device, sums):
        return sums + recv_ref[device]

    sums = lax.fori_loop(0, recv_ref.shape[0], returned, jnp.zeros((1, 256), F32), unroll=8)
    energy_ref[...] = eshort_ref[...] + long_ref[3:4]
    row8 = iota((8, 128), 0)
    lines3 = (sums[:, 0:128], pltpu.roll(jnp.broadcast_to(sums[:, 0:128], (8, 128)), 64, 1), sums[:, 128:256])
    lent = jnp.zeros((8, 128), F32)
    for axis in range(3):
        lent = jnp.where(row8 == axis, lines3[axis], lent)
    lent = jnp.where(iota((8, 128), 1) < 64, lent, 0.0)
    export = export_ref[...]
    twice = jnp.concatenate([export, export], axis=1)
    hot = jnp.where(iota((atoms, 128), 0) == twice, 1.0, 0.0).astype(BF16)
    high, low = split2(lent)
    rest = (lent - high.astype(F32) - low.astype(F32)).astype(BF16)
    back = mm_nt(high, hot) + mm_nt(low, hot) + mm_nt(rest, hot)
    for axis in range(3):
        total = long_ref[axis : axis + 1] + gown_ref[axis : axis + 1] + back[axis : axis + 1]
        forces_ref[axis : axis + 1] = -total


def cas_table(extent):
    indices = np.arange(extent)
    angle = (indices[:, None] * indices[None, :] % extent) * (2.0 * np.pi / extent)
    return (np.cos(angle) + np.sin(angle)) / np.sqrt(extent)


def halves(table):
    high = np.asarray(table, np.float32).astype(BF16)
    low = (np.asarray(table, np.float64) - high.astype(np.float64)).astype(np.float32).astype(BF16)
    return high, low


def wide(table):
    high, low = halves(table)
    return np.concatenate([high, high, low], axis=-1)


def wave_squares(extent):
    folded = (np.arange(extent) + extent // 2) % extent - extent // 2
    return (folded * (2.0 * np.pi / extent)) ** 2


def near(*arrays):
    return [pltpu.with_memory_space_constraint(array, pltpu.VMEM) for array in arrays]


def exchange(block, axis):
    size = lax.axis_size(axis)
    up = [(i, (i + 1) % size) for i in range(size)]
    if size <= 2:
        other = lax.ppermute(block, axis, up)
        return other, other
    return lax.ppermute(block, axis, up), lax.ppermute(block, axis, [(j, i) for i, j in up])


def per_device(
    atom_cell,
    atom_frac,
    features,
    ghost_export,
    neighbors,
    neighbor_count,
    w_up,
    radial_weight,
    w_out,
    energy_weight,
    charge_weight,
):
    channels, atoms = features.shape
    exported = ghost_export.shape[0]
    slots = neighbors.shape[1]
    counts = tuple(lax.axis_size(axis) for axis in MESH_AXES)
    count_x, count_y, count_z = counts
    devices = count_x * count_y * count_z
    half = channels // 2
    rows = channels + 16

    record, own, pq, info = pl.pallas_call(
        prep_kernel,
        out_shape=(
            pltpu.VMEM((half + 16, 2 * exported), BF16),
            pltpu.VMEM((rows, atoms), BF16),
            pltpu.VMEM((8, atoms), F32),
            pltpu.VMEM((devices, 1, 4 * atoms), F32),
        ),
        in_specs=[VMEM] * 6,
        out_specs=(VMEM,) * 4,
        scratch_shapes=[pltpu.VMEM((16, atoms), F32)],
        name="prep",
    )(features, atom_cell, atom_frac, ghost_export[None, :], w_up, charge_weight[None, :])

    info = lax.all_to_all(info, ("gx", "gy", "gz"), split_axis=0, concat_axis=0, tiled=True)
    grid_x, grid_y, grid_z = CX * count_x, CY * count_y, CZ * count_z
    grown_shape = ((grid_x + 3) * (grid_y + 8), grid_z)

    def spread(groups, *arrays):
        return pl.pallas_call(
            functools.partial(spread_kernel, counts, groups),
            out_shape=pltpu.VMEM(grown_shape, F32),
            in_specs=[VMEM] * len(arrays),
            out_specs=VMEM,
            scratch_shapes=[pltpu.VMEM((count_z, 256, atoms), F32)],
            compiler_params=PARAMS,
            name="spread",
        )(*near(*arrays))

    columns = count_x * count_y
    block = record[None]
    below, above = exchange(block, "gx")
    if count_x <= 2:
        block = jnp.concatenate([block, below], axis=0)
        x_of = (1, 0, 1)
    else:
        block = jnp.concatenate([below, block, above], axis=0)
        x_of = (0, 1, 2)
    below, above = exchange(block, "gy")
    grown = spread((0, columns // 2), info)
    below, above, grown = lax.optimization_barrier((below, above, grown))
    block = jnp.concatenate([below, block, above], axis=0)
    below, above = exchange(block, "gz")
    grown = spread((columns // 2, columns), info, grown)
    below, above, grown = lax.optimization_barrier((below, above, grown))

    domains = lent_domains(count_x)
    width = 256
    dense = 112
    all_tiles = -(-(atoms + len(domains) * exported) // 128)
    blocks = -(-all_tiles * 128 // width)
    send, gown, eshort = pl.pallas_call(
        functools.partial(short_kernel, (counts, x_of, exported, dense)),
        out_shape=(
            pltpu.VMEM((devices, 1, 256), F32),
            pltpu.VMEM((8, atoms), F32),
            pltpu.VMEM((1, atoms), F32),
        ),
        in_specs=[VMEM] * 11,
        out_specs=(VMEM,) * 3,
        scratch_shapes=[
            pltpu.VMEM((blocks * dense, width), BF16),
            pltpu.VMEM((channels - dense + 8, all_tiles * 128), F32),
            pltpu.VMEM((slots, width, atoms), BF16),
            pltpu.VMEM((slots, channels, atoms), BF16),
            pltpu.VMEM((slots, channels, atoms), F32),
            pltpu.VMEM((slots, 8, atoms), F32),
            pltpu.VMEM((slots, 8, atoms), F32),
            pltpu.VMEM((4, channels, atoms), F32),
            pltpu.VMEM((4, channels, atoms), BF16),
            pltpu.VMEM((slots, atoms), F32),
            pltpu.VMEM((slots, atoms), jnp.int32),
            pltpu.VMEM((blocks * 8, width), F32),
        ],
        compiler_params=PARAMS,
        name="short",
    )(
        *near(below, block, above, own),
        *near(neighbors.T, neighbor_count[None, :], pq, features),
        *near(radial_weight.T, w_out, energy_weight[None, :]),
    )

    recv = lax.all_to_all(send, ("gx", "gy", "gz"), split_axis=0, concat_axis=0, tiled=True)

    cas_x, cas_y, cas_z = cas_table(grid_x), cas_table(grid_y), cas_table(grid_z)
    square = (
        wave_squares(grid_x)[:, None, None] + wave_squares(grid_y)[None, :, None] + wave_squares(grid_z)[None, None, :]
    )
    safe = np.where(square > 0.0, square, 1.0)
    influence = np.where(square > 0.0, 4.0 * math.pi * np.exp(-square / (4.0 * ewald_beta_sq)) / safe, 0.0)
    influence = influence.reshape(grid_x * grid_y, grid_z).astype(np.float32)
    eye = np.eye(8)
    kx = wide(np.kron(cas_x, eye))
    x_rows = (np.arange(count_x)[:, None] * CX + np.arange(XL + 1)[None, :]) % grid_x
    kxo = np.stack([wide(np.kron(cas_x[r], eye)) for r in x_rows])
    y_rows = (np.arange(count_y)[:, None] * CY + np.arange(32)[None, :]) % grid_y
    hyo = np.stack([wide(cas_y[r]) for r in y_rows])
    z_rows = (np.arange(count_z)[:, None] * CZ + np.arange(128)[None, :]) % grid_z
    hzo = [halves(cas_z[:, r] * (np.arange(128) < ZL)[None, :]) for r in z_rows]
    hzoh, hzol = np.stack([t[0] for t in hzo]), np.stack([t[1] for t in hzo])
    hzh, hzl = halves(cas_z)

    far = pl.pallas_call(
        functools.partial(long_kernel, counts),
        out_shape=pltpu.VMEM((8, atoms), F32),
        in_specs=[VMEM] * 11,
        out_specs=VMEM,
        cost_estimate=pl.CostEstimate(flops=8_000_000_000, transcendentals=0, bytes_accessed=2_000_000),
        scratch_shapes=[
            pltpu.VMEM((grid_x * (grid_y + 8), grid_z), F32),
            pltpu.VMEM((grid_x * grid_y, grid_z), F32),
            pltpu.VMEM((XL * grid_y, grid_z), F32),
            pltpu.VMEM((XL * YL, 128), F32),
        ],
        compiler_params=PARAMS,
        name="long",
    )(
        *near(grown, pq),
        *near(*[jnp.asarray(t) for t in (wide(cas_y), hzh, hzl, kx, kxo, hyo, hzoh, hzol, influence)]),
    )
    forces, energy = pl.pallas_call(
        final_kernel,
        out_shape=(jax.ShapeDtypeStruct((3, atoms), F32), jax.ShapeDtypeStruct((1, atoms), F32)),
        in_specs=[VMEM] * 5,
        out_specs=(VMEM,) * 2,
        name="final",
    )(*near(recv, gown, eshort, far, ghost_export[None, :]))
    return (forces, energy.reshape(-1))


def solution(mesh):
    spread = ("gx", "gy", "gz")
    in_specs = (
        P(None, spread),
        P(None, spread),
        P(None, spread),
        P(spread),
        P(spread, None),
        P(spread),
        P(),
        P(),
        P(),
        P(),
        P(),
    )
    out_specs = (P(None, spread), P(spread))
    return jax.shard_map(per_device, mesh=mesh, in_specs=in_specs, out_specs=out_specs, check_vma=False)
```

```python
import functools
import math

import jax
import jax.numpy as jnp
import numpy as np
from jax import lax
from jax.experimental import pallas as pl
from jax.experimental.pallas import tpu as pltpu
from jax.sharding import PartitionSpec as P

CX = 8
CY = 16
CZ = 64
XL = CX + 3
YL = CY + 8
YW = CY + 4
ZL = CZ + 16

basis_step = 1.4
basis_width = 1.4
message_scale = 0.125
vector_scale = 1.0 / 6.0
ewald_beta_sq = 2.0

F32 = jnp.float32
BF16 = jnp.bfloat16
VMEM = pl.BlockSpec(memory_space=pltpu.VMEM)
SPREAD_EARLY = False
WAVE_EARLY = True
MESH_AXES = ("gx", "gy", "gz")
PARAMS = pltpu.CompilerParams(vmem_limit_bytes=24 * 1024 * 1024)


def iota(shape, dim):
    return lax.broadcasted_iota(jnp.int32, shape, dim)


def mm(a, b):
    return jnp.dot(a, b, preferred_element_type=F32)


def mm_nt(a, b):
    return lax.dot_general(a, b, (((1,), (1,)), ((), ())), preferred_element_type=F32)


def mm_tn(a, b):
    return lax.dot_general(a, b, (((0,), (0,)), ((), ())), preferred_element_type=F32)


def split2(values):
    high = values.astype(BF16)
    return high, (values - high.astype(F32)).astype(BF16)


def stack3(values):
    high, low = split2(values)
    return jnp.concatenate([high, low, high], axis=0)


def prep_kernel(feat_ref, cell_ref, frac_ref, export_ref, w_up_ref, cw_ref, rec_ref, own_ref, pq_ref, info_ref, p16_ref):
    channels, atoms = feat_ref.shape
    half = channels // 2
    exported = export_ref.shape[1]
    feat = feat_ref[...]
    up = mm(w_up_ref[...], feat).astype(BF16)
    charge = mm(jnp.broadcast_to(cw_ref[...], (16, channels)), feat)[0:1]
    cell = cell_ref[...].astype(F32)
    frac = frac_ref[...].astype(F32)
    p16_ref[...] = jnp.zeros_like(p16_ref)
    p16_ref[0:3] = cell
    p16_ref[8:11] = frac
    pq_ref[...] = jnp.zeros_like(pq_ref)
    pq_ref[0:3] = cell + frac
    pq_ref[3:4] = charge
    p16 = p16_ref[...].astype(BF16)
    own_ref[0:channels] = up
    own_ref[channels : channels + 16] = p16
    export = export_ref[...]
    twice = jnp.concatenate([export, export], axis=1)
    pick = jnp.where(iota((atoms, 2 * exported), 0) == twice, 1.0, 0.0).astype(BF16)
    first = mm(up[0:half], pick)
    second = mm(up[half:channels], pick)
    left = iota((half, 2 * exported), 1) < exported
    rec_ref[0:half] = jnp.where(left, first, second).astype(BF16)
    rec_ref[half : half + 16] = mm(p16, pick).astype(BF16)
    info = [pq_ref[r : r + 1, :] for r in range(4)]

    def fill(device, carry):
        for r in range(4):
            info_ref[device, :, r * atoms : (r + 1) * atoms] = info[r]
        return carry

    lax.fori_loop(0, info_ref.shape[0], fill, 0, unroll=8)


def lent_domains(count_x):
    around = [(b, c) for b in (-1, 0, 1) for c in (-1, 0, 1)]
    if count_x <= 2:
        return [(0, b, c) for b, c in around if (b, c) != (0, 0)] + [(1, b, c) for b, c in around]
    return [(a, b, c) for a in (-1, 0, 1) for b, c in around if (a, b, c) != (0, 0, 0)]


def short_kernel(
    setup,
    before_ref,
    mid_ref,
    after_ref,
    own_ref,
    nbr_ref,
    count_ref,
    pq_ref,
    feat_ref,
    rwt_ref,
    w_out_ref,
    ew_ref,
    send_ref,
    gown_ref,
    eshort_ref,
    table_ref,
    lanes_ref,
    hot_ref,
    upg_ref,
    msg_ref,
    rel_ref,
    bas_ref,
    sv_ref,
    svb_ref,
    shift_ref,
    col_ref,
    acc_ref,
):
    counts, x_of, exported, dense = setup
    count_x = counts[0]
    places = [lax.axis_index(axis) for axis in MESH_AXES]
    channels, atoms = feat_ref.shape
    half = channels // 2
    slots = nbr_ref.shape[0]
    width = table_ref.shape[1]
    blocks = table_ref.shape[0] // dense
    tiles = width // 128
    own_tiles = atoms // 128
    sparse = channels - dense
    all_tiles = lanes_ref.shape[1] // 128
    arrays = (before_ref, mid_ref, after_ref)
    per_axis = mid_ref.shape[0] // 3
    domains = lent_domains(count_x)

    def put(tile, up, pos):
        block, part = divmod(tile, tiles)
        lanes = slice(part * 128, (part + 1) * 128)
        for group in range(dense // 16):
            first = (group * blocks + block) * 16
            table_ref[first : first + 16, lanes] = up[group * 16 : group * 16 + 16].astype(BF16)
        lanes = slice(tile * 128, (tile + 1) * 128)
        if sparse:
            lanes_ref[0:sparse, lanes] = up[dense:channels]
        lanes_ref[sparse : sparse + 8, lanes] = pos

    last = blocks * tiles
    for tile in range(all_tiles, last):
        block, part = divmod(tile, tiles)
        for group in range(dense // 16):
            first = (group * blocks + block) * 16
            table_ref[first : first + 16, part * 128 : (part + 1) * 128] = jnp.zeros((16, 128), BF16)
    for tile in range(own_tiles):
        lanes = slice(tile * 128, (tile + 1) * 128)
        both = own_ref[:, lanes].astype(F32)
        put(tile, both[0:channels], both[channels : channels + 8] + both[channels + 8 : channels + 16])
    left64 = iota((half, 128), 1) < exported
    left16 = iota((16, 128), 1) < exported
    left8 = iota((8, 128), 1) < exported
    row8 = iota((8, 128), 0)
    for u in range(all_tiles - own_tiles):
        even = domains[2 * u]
        odd = domains[2 * u + 1] if 2 * u + 1 < len(domains) else None

        def record(domain):
            return arrays[domain[2] + 1][(domain[1] + 1) * per_axis + x_of[domain[0] + 1]].astype(F32)

        e = record(even)
        o = record(odd) if odd else jnp.zeros_like(e)
        odd = odd or (0, 0, 0)
        low = jnp.where(left64, e[0:half], pltpu.roll(o[0:half], 64, 1))
        high = jnp.where(left64, pltpu.roll(e[0:half], 64, 1), o[0:half])
        pos = jnp.where(left16, e[half : half + 16], o[half : half + 16])
        pos = pos[0:8] + pos[8:16]
        for axis, extent in ((1, CY), (2, CZ)):
            shift = jnp.where(left8, float(even[axis] * extent), float(odd[axis] * extent))
            pos = pos + jnp.where(row8 == axis, shift, 0.0)
        put(own_tiles + u, jnp.concatenate([low, high], axis=0), pos)

    index = nbr_ref[...]
    rank = index - atoms
    row = 9 * exported
    if count_x <= 2:
        inner = rank - row
        inner = jnp.where(inner >= 5 * exported, inner - exported, inner)
        outer = jnp.where(rank < row, rank, rank - 2 * row) + 8 * exported
        place = jnp.where(jnp.logical_and(rank >= row, rank < 2 * row), inner, outer)
    else:
        place = jnp.where(rank >= 14 * exported, rank - exported, rank)
    col_ref[...] = jnp.where(rank < 0, index, place + atoms)
    ahead = jnp.where(rank < row, -float(CX), jnp.where(rank < 2 * row, 0.0, float(CX)))
    shift_ref[...] = jnp.where(rank < 0, 0.0, ahead)

    row8 = iota((8, atoms), 0)
    own_pos = jnp.where(row8 < 3, pq_ref[...], 0.0)
    count = count_ref[...]
    centres = iota((8, atoms), 0).astype(F32) * basis_step
    table_row = iota((width, atoms), 0).astype(jnp.int16)
    rwt = rwt_ref[...]
    rwt_hi, rwt_lo = split2(rwt)
    rw3 = jnp.concatenate([rwt_hi.astype(F32), rwt_hi.astype(F32), rwt_lo.astype(F32), jnp.zeros_like(rwt)], axis=0)
    rw3 = jnp.transpose(jnp.concatenate([rw3, jnp.zeros((96, channels), F32)], axis=0))[:, 0:32].astype(BF16)

    def gather(k):
        col = col_ref[pl.ds(k, 1), :]
        low = col % width
        high = col // width
        hot = jnp.where(table_row == low.astype(jnp.int16), jnp.ones((), BF16), jnp.zeros((), BF16))
        hot_ref[k] = hot
        got = mm(table_ref[...], hot)
        first = []
        for group in range(dense // 16):
            rows = [got[(group * blocks + block) * 16 : (group * blocks + block + 1) * 16] for block in range(blocks)]
            value = rows[0]
            for block in range(1, blocks):
                value = jnp.where(high == block, rows[block], value)
            first.append(value)
        halves_ = []
        for part in range(own_tiles):
            lanes = slice(part * 128, (part + 1) * 128)
            within = jnp.broadcast_to((col % 128)[:, lanes], (8, 128))
            which = jnp.broadcast_to((col // 128)[:, lanes], (8, 128))
            found = [None] * (sparse // 8 + 1)
            for tile in range(all_tiles):
                here = which == tile
                for c in range(sparse // 8 + 1):
                    piece = lanes_ref[c * 8 : (c + 1) * 8, tile * 128 : (tile + 1) * 128]
                    piece = jnp.take_along_axis(piece, within, axis=1)
                    found[c] = piece if tile == 0 else jnp.where(here, piece, found[c])
            halves_.append(jnp.concatenate(found, axis=0))
        second = jnp.concatenate(halves_, axis=1)
        up = jnp.concatenate(first + ([second[0:sparse]] if sparse else []), axis=0)
        upg_ref[k] = up.astype(BF16)
        rel = second[sparse : sparse + 8] - own_pos
        rel = rel + jnp.where(row8 == 0, shift_ref[pl.ds(k, 1), :], 0.0)
        dist = jnp.sqrt(jnp.sum(rel * rel, axis=0, keepdims=True) + 1.0)
        rel_ref[k] = jnp.where(row8 == 3, dist, rel)
        scaled = (dist - centres) * (1.0 / basis_width)
        basis = jnp.where(k < count, jnp.exp(-(scaled * scaled)), 0.0)
        bas_ref[k] = basis
        b_hi = basis.astype(BF16).astype(F32)
        b_lo = basis - b_hi
        stacked = jnp.concatenate([b_hi, b_lo, b_hi, jnp.zeros_like(b_hi)], axis=0).astype(BF16)
        message = mm(rw3, stacked) * up
        msg_ref[k] = message
        return message, rel

    part = 16
    stride = math.gcd(slots, 8)
    sv_ref[...] = jnp.zeros_like(sv_ref)

    def gather_some(number, carry):
        found = [gather(number * stride + step) for step in range(stride)]
        for first in range(0, channels, part):
            sums = [sv_ref[axis, first : first + part] for axis in range(4)]
            for step in range(stride):
                message = msg_ref[number * stride + step, first : first + part]
                rel = found[step][1]
                sums[0] = sums[0] + message
                for axis in range(3):
                    sums[axis + 1] = sums[axis + 1] + message * rel[axis : axis + 1]
            for axis in range(4):
                sv_ref[axis, first : first + part] = sums[axis]
        return carry

    lax.fori_loop(0, slots // stride, gather_some, 0)

    scalar = sv_ref[0] * message_scale
    vectors = [sv_ref[axis + 1] * (message_scale * vector_scale) for axis in range(3)]
    invariant = scalar + scalar * scalar + (vectors[0] * vectors[0] + vectors[1] * vectors[1] + vectors[2] * vectors[2])
    w_out = w_out_ref[...]
    hidden = feat_ref[...].astype(F32) + mm(w_out, invariant.astype(BF16))
    square = iota((channels, channels), 0) == iota((channels, channels), 1)
    ew = jnp.sum(jnp.where(square, ew_ref[...].astype(F32), 0.0), axis=1, keepdims=True)
    gate = 1.0 / (1.0 + jnp.exp(-hidden))
    eshort_ref[...] = jnp.sum(ew * (hidden * gate), axis=0, keepdims=True)
    d_hidden = ew * (gate * (1.0 + hidden * (1.0 - gate)))
    dh_hi, dh_lo = split2(d_hidden)
    d_inv = (mm_tn(w_out, dh_hi) + mm_tn(w_out, dh_lo)).astype(BF16).astype(F32)
    for axis in range(4):
        factor = (1.0 + 2.0 * scalar) * message_scale if axis == 0 else vectors[axis - 1] * (2.0 * message_scale * vector_scale)
        sv_ref[axis] = d_inv * factor
        svb_ref[axis] = (d_inv * factor).astype(BF16)

    acc_ref[...] = jnp.zeros_like(acc_ref)
    reduce_left = jnp.concatenate([rwt_hi.astype(F32), rwt_lo.astype(F32)], axis=0).astype(BF16)
    chunk = 32

    def scatter(k, total):
        rel8 = rel_ref[k]
        basis = bas_ref[k]
        dist = rel8[3:4]
        rel_low = [rel8[axis : axis + 1].astype(BF16) for axis in range(3)]
        turns = [jnp.zeros((8, atoms), F32) for _ in range(3)]
        right = []
        for first in range(0, channels, chunk):
            at = slice(first, first + chunk)
            message = msg_ref[k, at, :]
            pull = svb_ref[0, at, :]
            for axis in range(3):
                pull = pull + svb_ref[axis + 1, at, :] * rel_low[axis]
                turn = sv_ref[axis + 1, at, :] * message
                for r in range(0, chunk, 8):
                    turns[axis] = turns[axis] + turn[r : r + 8]
            right.append(pull * upg_ref[k, at, :])
        sums = mm(reduce_left, jnp.concatenate(right, axis=0))
        d_basis = sums[0:8] + sums[8:16]
        slope = d_basis * basis * ((dist - centres) * (-2.0 / (basis_width * basis_width)))
        d_dist = jnp.sum(slope, axis=0, keepdims=True) / dist
        d_rel = jnp.where(row8 < 3, d_dist * rel8, 0.0)
        for axis in range(3):
            d_rel = d_rel + jnp.where(row8 == axis, jnp.sum(turns[axis], axis=0, keepdims=True), 0.0)
        d_hi = d_rel.astype(BF16).astype(F32)
        both = d_hi + pltpu.roll(d_rel - d_hi, 4, 0)
        high = col_ref[pl.ds(k, 1), :] // width
        left = jnp.concatenate([jnp.where(high == block, both, 0.0) for block in range(blocks)], axis=0)
        acc_ref[...] += mm_nt(left.astype(BF16), hot_ref[k])
        return total + d_rel

    total = lax.fori_loop(0, slots, scatter, jnp.zeros((8, atoms), F32), unroll=4)

    def grad_tile(tile):
        block, piece = divmod(tile, tiles)
        g = acc_ref[block * 8 : block * 8 + 8, piece * 128 : (piece + 1) * 128]
        return g + pltpu.roll(g, 4, 0)

    for tile in range(own_tiles):
        gown_ref[:, tile * 128 : (tile + 1) * 128] = grad_tile(tile) - total[:, tile * 128 : (tile + 1) * 128]

    send_ref[...] = jnp.zeros_like(send_ref)
    left1 = iota((1, 128), 1) < exported
    for u in range(all_tiles - own_tiles):
        g = grad_tile(own_tiles + u)
        swapped = pltpu.roll(g, 64, 1)
        for side in range(2):
            if 2 * u + side >= len(domains):
                continue
            a, b, c = domains[2 * u + side]
            device = lax.rem(places[0] + (a + counts[0]), counts[0]) * counts[1]
            device = (device + lax.rem(places[1] + (b + counts[1]), counts[1])) * counts[2]
            device = device + lax.rem(places[2] + (c + counts[2]), counts[2])
            here, there = (g, swapped) if side == 0 else (swapped, g)
            top = jnp.where(left1, here[0:1], there[1:2])
            bottom = jnp.where(left1, here[2:3], 0.0)
            send_ref[device, :, 0:128] += top
            send_ref[device, :, 128:256] += bottom


def spline(distance):
    outer = jnp.maximum(2.0 - distance, 0.0)
    inner = jnp.maximum(1.0 - distance, 0.0)
    return outer * outer * outer * (1.0 / 6.0) - inner * inner * inner * (4.0 / 6.0)


def weights_of(count, position):
    gap = (iota((count, position.shape[1]), 0) - 1).astype(F32) - position
    return spline(jnp.abs(gap))


def slopes_of(count, position):
    gap = (iota((count, position.shape[1]), 0) - 1).astype(F32) - position
    distance = jnp.abs(gap)
    outer = jnp.maximum(2.0 - distance, 0.0)
    inner = jnp.maximum(1.0 - distance, 0.0)
    size = outer * outer * 0.5 - inner * inner * 2.0
    return jnp.where(gap > 0.0, size, -size)


def spread_kernel(counts, info_ref, rho_ref, plane_ref):
    count_x, count_y, count_z = counts
    atoms = info_ref.shape[2] // 4
    tall = CY * count_y + 8
    rho_ref[...] = jnp.zeros_like(rho_ref)
    plane_ref[...] = jnp.zeros_like(plane_ref)

    def domain(number, slot):
        info = info_ref[number]
        wx = weights_of(16, info[:, 0:atoms]) * info[:, 3 * atoms : 4 * atoms]
        even = weights_of(24, info[:, atoms : 2 * atoms])
        odd = pltpu.roll(even, 4, 0)
        for x in range(0, XL, 2):
            first = x * YW
            here = wx[x : x + 1]
            plane_ref[slot, first : first + 16] = here * even[0:16]
            if x + 1 == XL:
                plane_ref[slot, first + 16 : first + 24] = here * even[16:24]
                continue
            there = wx[x + 1 : x + 2]
            plane_ref[slot, first + 16 : first + 24] = here * even[16:24] + there * odd[0:8]
            plane_ref[slot, first + 24 : first + 40] = there * odd[8:24]
        high, low = split2(weights_of(ZL, info[:, 2 * atoms : 3 * atoms]))
        plane_high, plane_low = split2(plane_ref[slot])
        both = mm_nt(jnp.concatenate([high, low], axis=0), plane_high)
        return both[0:ZL] + both[ZL : 2 * ZL] + mm_nt(high, plane_low)

    def spread(group, carry):
        grown = [domain(group * count_z + l, l % plane_ref.shape[0]) for l in range(count_z)]
        pieces = []
        for l in range(count_z):
            pieces.append(grown[l][0 : ZL - CZ] + grown[l - 1][CZ:ZL])
            pieces.append(grown[l][ZL - CZ : CZ])
        turned = jnp.transpose(jnp.concatenate(pieces, axis=0))
        first = (group // count_y * CX) * tall + (group % count_y) * CY
        for x in range(XL):
            at = pl.ds(pl.multiple_of(first + x * tall, 8), YW)
            rho_ref[at, :] += turned[x * YW : (x + 1) * YW]
        return carry

    lax.fori_loop(0, count_x * count_y, spread, 0)


def times_z(values, table_high, table_low):
    high, low = split2(values)
    return mm(high, table_high) + mm(high, table_low) + mm(low, table_high)


def wave_kernel(
    counts,
    grown_ref,
    hy_ref,
    hzh_ref,
    hzl_ref,
    kx_ref,
    kxo_ref,
    influence_ref,
    back_ref,
    rho_ref,
    spec_ref,
):
    count_x, count_y, _ = counts
    grid_x, grid_y = CX * count_x, CY * count_y
    tall = grid_y + 8
    rho_ref[...] = grown_ref[0 : grid_x * tall]
    place_x = lax.axis_index("gx")
    for x in range(3):
        rho_ref[x * tall : (x + 1) * tall] += grown_ref[(grid_x + x) * tall : (grid_x + x + 1) * tall]

    def along_yz(x, carry):
        start = pl.multiple_of(x * tall, 8)
        top = rho_ref[pl.ds(start, 8), :] + rho_ref[pl.ds(start + grid_y, 8), :]
        values = jnp.concatenate([top, rho_ref[pl.ds(start + 8, grid_y - 8), :]], axis=0)
        turned = mm(hy_ref[...], stack3(values))
        spec_ref[pl.ds(pl.multiple_of(x * grid_y, 8), grid_y), :] = times_z(turned, hzh_ref[...], hzl_ref[...])
        return carry

    lax.fori_loop(0, grid_x, along_yz, 0, unroll=4)

    def along_x(octet, carry):
        def part(ref, x):
            return ref[pl.ds(pl.multiple_of(x * grid_y + octet * 8, 8), 8), :]

        values = jnp.concatenate([part(spec_ref, x) for x in range(grid_x)], axis=0)
        factor = jnp.concatenate([part(influence_ref, x) for x in range(grid_x)], axis=0)
        back = mm(kxo_ref[place_x], stack3(mm(kx_ref[...], stack3(values)) * factor))
        for x in range(XL):
            back_ref[pl.ds(pl.multiple_of(x * grid_y + octet * 8, 8), 8), :] = back[x * 8 : (x + 1) * 8]
        return carry

    lax.fori_loop(0, grid_y // 8, along_x, 0, unroll=2)


def field_kernel(counts, back_ref, pq_ref, hyo_ref, hzoh_ref, hzol_ref, out_ref, phi_ref):
    grid_y = CY * counts[1]
    atoms = pq_ref.shape[1]
    place_y, place_z = [lax.axis_index(axis) for axis in MESH_AXES[1:]]
    for x in range(XL):
        turned = mm(hyo_ref[place_y], stack3(back_ref[x * grid_y : (x + 1) * grid_y]))
        phi_ref[x * YL : (x + 1) * YL] = times_z(turned, hzoh_ref[place_z], hzol_ref[place_z])[0:YL]

    own = pq_ref[...]
    charge = own[3:4]
    wx, dx = weights_of(16, own[0:1]), slopes_of(16, own[0:1])
    wy, dy = weights_of(YL, own[1:2]), slopes_of(YL, own[1:2])
    wzh, wzl = split2(jnp.concatenate([weights_of(128, own[2:3]), slopes_of(128, own[2:3])], axis=1))
    high, low = split2(phi_ref[...])
    lines = mm(high, wzh) + mm(high, wzl) + mm(low, wzh)
    potential = jnp.zeros((1, atoms), F32)
    field = [jnp.zeros((1, atoms), F32) for _ in range(3)]
    for x in range(XL):
        flat = lines[x * YL : (x + 1) * YL, 0:atoms]
        steep = lines[x * YL : (x + 1) * YL, atoms : 2 * atoms]
        s0 = jnp.sum(wy * flat, axis=0, keepdims=True)
        sy = jnp.sum(dy * flat, axis=0, keepdims=True)
        sz = jnp.sum(wy * steep, axis=0, keepdims=True)
        here = wx[x : x + 1]
        potential = potential + here * s0
        field[0] = field[0] + dx[x : x + 1] * s0
        field[1] = field[1] + here * sy
        field[2] = field[2] + here * sz
    out_ref[...] = jnp.zeros_like(out_ref)
    for axis in range(3):
        out_ref[axis : axis + 1] = charge * field[axis]
    out_ref[3:4] = 0.5 * charge * potential


def final_kernel(recv_ref, gown_ref, eshort_ref, long_ref, export_ref, forces_ref, energy_ref):
    atoms = gown_ref.shape[1]

    def returned(device, sums):
        return sums + recv_ref[device]

    sums = lax.fori_loop(0, recv_ref.shape[0], returned, jnp.zeros((1, 256), F32), unroll=8)
    energy_ref[...] = eshort_ref[...] + long_ref[3:4]
    row8 = iota((8, 128), 0)
    lines3 = (sums[:, 0:128], pltpu.roll(jnp.broadcast_to(sums[:, 0:128], (8, 128)), 64, 1), sums[:, 128:256])
    lent = jnp.zeros((8, 128), F32)
    for axis in range(3):
        lent = jnp.where(row8 == axis, lines3[axis], lent)
    lent = jnp.where(iota((8, 128), 1) < 64, lent, 0.0)
    export = export_ref[...]
    twice = jnp.concatenate([export, export], axis=1)
    hot = jnp.where(iota((atoms, 128), 0) == twice, 1.0, 0.0).astype(BF16)
    high, low = split2(lent)
    rest = (lent - high.astype(F32) - low.astype(F32)).astype(BF16)
    back = mm_nt(high, hot) + mm_nt(low, hot) + mm_nt(rest, hot)
    for axis in range(3):
        total = long_ref[axis : axis + 1] + gown_ref[axis : axis + 1] + back[axis : axis + 1]
        forces_ref[axis : axis + 1] = -total


def cas_table(extent):
    indices = np.arange(extent)
    angle = (indices[:, None] * indices[None, :] % extent) * (2.0 * np.pi / extent)
    return (np.cos(angle) + np.sin(angle)) / np.sqrt(extent)


def halves(table):
    high = np.asarray(table, np.float32).astype(BF16)
    low = (np.asarray(table, np.float64) - high.astype(np.float64)).astype(np.float32).astype(BF16)
    return high, low


def wide(table):
    high, low = halves(table)
    return np.concatenate([high, high, low], axis=-1)


def wave_squares(extent):
    folded = (np.arange(extent) + extent // 2) % extent - extent // 2
    return (folded * (2.0 * np.pi / extent)) ** 2


def near(*arrays):
    return [pltpu.with_memory_space_constraint(array, pltpu.VMEM) for array in arrays]


def exchange(block, axes, offsets):
    sizes = [lax.axis_size(axis) for axis in axes]
    moves = []
    for source in np.ndindex(*sizes):
        target = [(place + step) % size for place, step, size in zip(source, offsets, sizes)]
        moves.append((int(np.ravel_multi_index(source, sizes)), int(np.ravel_multi_index(target, sizes))))
    return lax.ppermute(block, axes, moves)


def per_device(
    atom_cell,
    atom_frac,
    features,
    ghost_export,
    neighbors,
    neighbor_count,
    w_up,
    radial_weight,
    w_out,
    energy_weight,
    charge_weight,
):
    channels, atoms = features.shape
    exported = ghost_export.shape[0]
    slots = neighbors.shape[1]
    counts = tuple(lax.axis_size(axis) for axis in MESH_AXES)
    count_x, count_y, count_z = counts
    devices = count_x * count_y * count_z
    half = channels // 2
    rows = channels + 16

    record, own, pq, info = pl.pallas_call(
        prep_kernel,
        out_shape=(
            pltpu.VMEM((half + 16, 2 * exported), BF16),
            pltpu.VMEM((rows, atoms), BF16),
            pltpu.VMEM((8, atoms), F32),
            pltpu.VMEM((devices, 1, 4 * atoms), F32),
        ),
        in_specs=[VMEM] * 6,
        out_specs=(VMEM,) * 4,
        scratch_shapes=[pltpu.VMEM((16, atoms), F32)],
        name="prep",
    )(features, atom_cell, atom_frac, ghost_export[None, :], w_up, charge_weight[None, :])

    info = lax.all_to_all(info, MESH_AXES, split_axis=0, concat_axis=0, tiled=True)
    grid_x, grid_y, grid_z = CX * count_x, CY * count_y, CZ * count_z
    cas_x, cas_y, cas_z = cas_table(grid_x), cas_table(grid_y), cas_table(grid_z)
    square = (
        wave_squares(grid_x)[:, None, None] + wave_squares(grid_y)[None, :, None] + wave_squares(grid_z)[None, None, :]
    )
    safe = np.where(square > 0.0, square, 1.0)
    influence = np.where(square > 0.0, 4.0 * math.pi * np.exp(-square / (4.0 * ewald_beta_sq)) / safe, 0.0)
    influence = influence.reshape(grid_x * grid_y, grid_z).astype(np.float32)
    eye = np.eye(8)
    kx = wide(np.kron(cas_x, eye))
    x_rows = (np.arange(count_x)[:, None] * CX + np.arange(XL + 1)[None, :]) % grid_x
    kxo = np.stack([wide(np.kron(cas_x[r], eye)) for r in x_rows])
    y_rows = (np.arange(count_y)[:, None] * CY + np.arange(32)[None, :]) % grid_y
    hyo = np.stack([wide(cas_y[r]) for r in y_rows])
    z_rows = (np.arange(count_z)[:, None] * CZ + np.arange(128)[None, :]) % grid_z
    hzo = [halves(cas_z[:, r] * (np.arange(128) < ZL)[None, :]) for r in z_rows]
    hzoh, hzol = np.stack([t[0] for t in hzo]), np.stack([t[1] for t in hzo])
    hzh, hzl = halves(cas_z)

    grown_shape = ((grid_x + 3) * (grid_y + 8), grid_z)

    block = record[None]
    if count_x <= 2:
        block = jnp.concatenate([block, exchange(block, ("gx",), (1,))], axis=0)
        x_of = (1, 0, 1)
    else:
        sides = [exchange(block, ("gx",), (step,)) for step in (1, -1)]
        block = jnp.concatenate([sides[0], block, sides[1]], axis=0)
        x_of = (0, 1, 2)
    below = exchange(block, ("gy",), (1,))
    above = exchange(block, ("gy",), (-1,))
    grown = pl.pallas_call(
        functools.partial(spread_kernel, counts),
        out_shape=pltpu.VMEM(grown_shape, F32),
        in_specs=[VMEM],
        out_specs=VMEM,
        scratch_shapes=[pltpu.VMEM((count_z, 256, atoms), F32)],
        compiler_params=PARAMS,
        name="spread",
    )(*near(info))
    if SPREAD_EARLY:
        below, above, grown = lax.optimization_barrier((below, above, grown))
    block = jnp.concatenate([below, block, above], axis=0)
    below = exchange(block, ("gz",), (1,))
    above = exchange(block, ("gz",), (-1,))
    if WAVE_EARLY:
        below, above, grown = lax.optimization_barrier((below, above, grown))
    waves = pl.pallas_call(
        functools.partial(wave_kernel, counts),
        out_shape=pltpu.VMEM((XL * grid_y, grid_z), F32),
        in_specs=[VMEM] * 7,
        out_specs=VMEM,
        scratch_shapes=[
            pltpu.VMEM((grid_x * (grid_y + 8), grid_z), F32),
            pltpu.VMEM((grid_x * grid_y, grid_z), F32),
        ],
        compiler_params=PARAMS,
        name="wave",
    )(*near(grown, *[jnp.asarray(t) for t in (wide(cas_y), hzh, hzl, kx, kxo, influence)]))

    domains = lent_domains(count_x)
    width = 256
    dense = 112
    all_tiles = -(-(atoms + len(domains) * exported) // 128)
    blocks = -(-all_tiles * 128 // width)
    send, gown, eshort = pl.pallas_call(
        functools.partial(short_kernel, (counts, x_of, exported, dense)),
        out_shape=(
            pltpu.VMEM((devices, 1, 256), F32),
            pltpu.VMEM((8, atoms), F32),
            pltpu.VMEM((1, atoms), F32),
        ),
        in_specs=[VMEM] * 11,
        out_specs=(VMEM,) * 3,
        scratch_shapes=[
            pltpu.VMEM((blocks * dense, width), BF16),
            pltpu.VMEM((channels - dense + 8, all_tiles * 128), F32),
            pltpu.VMEM((slots, width, atoms), BF16),
            pltpu.VMEM((slots, channels, atoms), BF16),
            pltpu.VMEM((slots, channels, atoms), F32),
            pltpu.VMEM((slots, 8, atoms), F32),
            pltpu.VMEM((slots, 8, atoms), F32),
            pltpu.VMEM((4, channels, atoms), F32),
            pltpu.VMEM((4, channels, atoms), BF16),
            pltpu.VMEM((slots, atoms), F32),
            pltpu.VMEM((slots, atoms), jnp.int32),
            pltpu.VMEM((blocks * 8, width), F32),
        ],
        compiler_params=PARAMS,
        name="short",
    )(
        *near(below, block, above, own),
        *near(neighbors.T, neighbor_count[None, :], pq, features),
        *near(radial_weight.T, w_out, energy_weight[None, :]),
    )

    recv = lax.all_to_all(send, MESH_AXES, split_axis=0, concat_axis=0, tiled=True)

    far = pl.pallas_call(
        functools.partial(field_kernel, counts),
        out_shape=pltpu.VMEM((8, atoms), F32),
        in_specs=[VMEM] * 5,
        out_specs=VMEM,
        scratch_shapes=[pltpu.VMEM((XL * YL, 128), F32)],
        compiler_params=PARAMS,
        name="field",
    )(*near(waves, pq, jnp.asarray(hyo), jnp.asarray(hzoh), jnp.asarray(hzol)))
    forces, energy = pl.pallas_call(
        final_kernel,
        out_shape=(jax.ShapeDtypeStruct((3, atoms), F32), jax.ShapeDtypeStruct((1, atoms), F32)),
        in_specs=[VMEM] * 5,
        out_specs=(VMEM,) * 2,
        name="final",
    )(*near(recv, gown, eshort, far, ghost_export[None, :]))
    return (forces, energy.reshape(-1))


def solution(mesh):
    spread = ("gx", "gy", "gz")
    in_specs = (
        P(None, spread),
        P(None, spread),
        P(None, spread),
        P(spread),
        P(spread, None),
        P(spread),
        P(),
        P(),
        P(),
        P(),
        P(),
    )
    out_specs = (P(None, spread), P(spread))

    return jax.shard_map(per_device, mesh=mesh, in_specs=in_specs, out_specs=out_specs, check_vma=False)
```

```python
import functools
import math

import jax
import jax.numpy as jnp
import numpy as np
from jax import lax
from jax.experimental import pallas as pl
from jax.experimental.pallas import tpu as pltpu
from jax.sharding import PartitionSpec as P

CX = 8
CY = 16
CZ = 64
XL = CX + 3
YL = CY + 8
YW = CY + 4
XW = XL * YW + 4
ZL = CZ + 16

basis_step = 1.4
basis_width = 1.4
message_scale = 0.125
vector_scale = 1.0 / 6.0
ewald_beta_sq = 2.0

F32 = jnp.float32
BF16 = jnp.bfloat16
VMEM = pl.BlockSpec(memory_space=pltpu.VMEM)
SPREAD_EARLY = False
WAVE_EARLY = True
MESH_AXES = ("gx", "gy", "gz")
PARAMS = pltpu.CompilerParams(vmem_limit_bytes=24 * 1024 * 1024)


def iota(shape, dim):
    return lax.broadcasted_iota(jnp.int32, shape, dim)


def mm(a, b):
    return jnp.dot(a, b, preferred_element_type=F32)


def mm_nt(a, b):
    return lax.dot_general(a, b, (((1,), (1,)), ((), ())), preferred_element_type=F32)


def mm_tn(a, b):
    return lax.dot_general(a, b, (((0,), (0,)), ((), ())), preferred_element_type=F32)


def split2(values):
    high = values.astype(BF16)
    return high, (values - high.astype(F32)).astype(BF16)


def stack3(values):
    high, low = split2(values)
    return jnp.concatenate([high, low, high], axis=0)


def prep_kernel(feat_ref, cell_ref, frac_ref, export_ref, w_up_ref, cw_ref, rec_ref, own_ref, pq_ref, info_ref, p16_ref):
    channels, atoms = feat_ref.shape
    half = channels // 2
    exported = export_ref.shape[1]
    feat = feat_ref[...]
    up = mm(w_up_ref[...], feat).astype(BF16)
    charge = mm(jnp.broadcast_to(cw_ref[...], (16, channels)), feat)[0:1]
    cell = cell_ref[...].astype(F32)
    frac = frac_ref[...].astype(F32)
    p16_ref[...] = jnp.zeros_like(p16_ref)
    p16_ref[0:3] = cell
    p16_ref[8:11] = frac
    pq_ref[...] = jnp.zeros_like(pq_ref)
    pq_ref[0:3] = cell + frac
    pq_ref[3:4] = charge
    p16 = p16_ref[...].astype(BF16)
    own_ref[0:channels] = up
    own_ref[channels : channels + 16] = p16
    export = export_ref[...]
    twice = jnp.concatenate([export, export], axis=1)
    pick = jnp.where(iota((atoms, 2 * exported), 0) == twice, 1.0, 0.0).astype(BF16)
    first = mm(up[0:half], pick)
    second = mm(up[half:channels], pick)
    left = iota((half, 2 * exported), 1) < exported
    rec_ref[0:half] = jnp.where(left, first, second).astype(BF16)
    rec_ref[half : half + 16] = mm(p16, pick).astype(BF16)
    info = [pq_ref[r : r + 1, :] for r in range(4)]

    def fill(device, carry):
        for r in range(4):
            info_ref[device, :, r * atoms : (r + 1) * atoms] = info[r]
        return carry

    lax.fori_loop(0, info_ref.shape[0], fill, 0, unroll=8)


def lent_domains(count_x):
    around = [(b, c) for b in (-1, 0, 1) for c in (-1, 0, 1)]
    if count_x <= 2:
        return [(0, b, c) for b, c in around if (b, c) != (0, 0)] + [(1, b, c) for b, c in around]
    return [(a, b, c) for a in (-1, 0, 1) for b, c in around if (a, b, c) != (0, 0, 0)]


def short_kernel(
    setup,
    before_ref,
    mid_ref,
    after_ref,
    own_ref,
    nbr_ref,
    count_ref,
    pq_ref,
    feat_ref,
    rwt_ref,
    w_out_ref,
    ew_ref,
    send_ref,
    gown_ref,
    eshort_ref,
    table_ref,
    lanes_ref,
    hot_ref,
    upg_ref,
    msg_ref,
    rel_ref,
    bas_ref,
    sv_ref,
    svb_ref,
    shift_ref,
    col_ref,
    acc_ref,
):
    counts, x_of, exported, dense = setup
    count_x = counts[0]
    places = [lax.axis_index(axis) for axis in MESH_AXES]
    channels, atoms = feat_ref.shape
    half = channels // 2
    slots = nbr_ref.shape[0]
    width = table_ref.shape[1]
    blocks = table_ref.shape[0] // dense
    tiles = width // 128
    own_tiles = atoms // 128
    sparse = channels - dense
    all_tiles = lanes_ref.shape[1] // 128
    arrays = (before_ref, mid_ref, after_ref)
    per_axis = mid_ref.shape[0] // 3
    domains = lent_domains(count_x)

    def put(tile, up, pos):
        block, part = divmod(tile, tiles)
        lanes = slice(part * 128, (part + 1) * 128)
        for group in range(dense // 16):
            first = (group * blocks + block) * 16
            table_ref[first : first + 16, lanes] = up[group * 16 : group * 16 + 16].astype(BF16)
        lanes = slice(tile * 128, (tile + 1) * 128)
        if sparse:
            lanes_ref[0:sparse, lanes] = up[dense:channels]
        lanes_ref[sparse : sparse + 8, lanes] = pos

    last = blocks * tiles
    for tile in range(all_tiles, last):
        block, part = divmod(tile, tiles)
        for group in range(dense // 16):
            first = (group * blocks + block) * 16
            table_ref[first : first + 16, part * 128 : (part + 1) * 128] = jnp.zeros((16, 128), BF16)
    for tile in range(own_tiles):
        lanes = slice(tile * 128, (tile + 1) * 128)
        both = own_ref[:, lanes].astype(F32)
        put(tile, both[0:channels], both[channels : channels + 8] + both[channels + 8 : channels + 16])
    left64 = iota((half, 128), 1) < exported
    left16 = iota((16, 128), 1) < exported
    left8 = iota((8, 128), 1) < exported
    row8 = iota((8, 128), 0)
    for u in range(all_tiles - own_tiles):
        even = domains[2 * u]
        odd = domains[2 * u + 1] if 2 * u + 1 < len(domains) else None

        def record(domain):
            return arrays[domain[2] + 1][(domain[1] + 1) * per_axis + x_of[domain[0] + 1]].astype(F32)

        e = record(even)
        o = record(odd) if odd else jnp.zeros_like(e)
        odd = odd or (0, 0, 0)
        low = jnp.where(left64, e[0:half], pltpu.roll(o[0:half], 64, 1))
        high = jnp.where(left64, pltpu.roll(e[0:half], 64, 1), o[0:half])
        pos = jnp.where(left16, e[half : half + 16], o[half : half + 16])
        pos = pos[0:8] + pos[8:16]
        for axis, extent in ((1, CY), (2, CZ)):
            shift = jnp.where(left8, float(even[axis] * extent), float(odd[axis] * extent))
            pos = pos + jnp.where(row8 == axis, shift, 0.0)
        put(own_tiles + u, jnp.concatenate([low, high], axis=0), pos)

    index = nbr_ref[...]
    rank = index - atoms
    row = 9 * exported
    if count_x <= 2:
        inner = rank - row
        inner = jnp.where(inner >= 5 * exported, inner - exported, inner)
        outer = jnp.where(rank < row, rank, rank - 2 * row) + 8 * exported
        place = jnp.where(jnp.logical_and(rank >= row, rank < 2 * row), inner, outer)
    else:
        place = jnp.where(rank >= 14 * exported, rank - exported, rank)
    col_ref[...] = jnp.where(rank < 0, index, place + atoms)
    ahead = jnp.where(rank < row, -float(CX), jnp.where(rank < 2 * row, 0.0, float(CX)))
    shift_ref[...] = jnp.where(rank < 0, 0.0, ahead)

    row8 = iota((8, atoms), 0)
    own_pos = jnp.where(row8 < 3, pq_ref[...], 0.0)
    count = count_ref[...]
    centres = iota((8, atoms), 0).astype(F32) * basis_step
    table_row = iota((width, atoms), 0).astype(jnp.int16)
    rwt = rwt_ref[...]
    rwt_hi, rwt_lo = split2(rwt)
    rw3 = jnp.concatenate([rwt_hi.astype(F32), rwt_hi.astype(F32), rwt_lo.astype(F32), jnp.zeros_like(rwt)], axis=0)
    rw3 = jnp.transpose(jnp.concatenate([rw3, jnp.zeros((96, channels), F32)], axis=0))[:, 0:32].astype(BF16)

    def gather(k):
        col = col_ref[pl.ds(k, 1), :]
        low = col % width
        high = col // width
        hot = jnp.where(table_row == low.astype(jnp.int16), jnp.ones((), BF16), jnp.zeros((), BF16))
        hot_ref[k] = hot
        got = mm(table_ref[...], hot)
        first = []
        for group in range(dense // 16):
            rows = [got[(group * blocks + block) * 16 : (group * blocks + block + 1) * 16] for block in range(blocks)]
            value = rows[0]
            for block in range(1, blocks):
                value = jnp.where(high == block, rows[block], value)
            first.append(value)
        halves_ = []
        for part in range(own_tiles):
            lanes = slice(part * 128, (part + 1) * 128)
            within = jnp.broadcast_to((col % 128)[:, lanes], (8, 128))
            which = jnp.broadcast_to((col // 128)[:, lanes], (8, 128))
            found = [None] * (sparse // 8 + 1)
            for tile in range(all_tiles):
                here = which == tile
                for c in range(sparse // 8 + 1):
                    piece = lanes_ref[c * 8 : (c + 1) * 8, tile * 128 : (tile + 1) * 128]
                    piece = jnp.take_along_axis(piece, within, axis=1)
                    found[c] = piece if tile == 0 else jnp.where(here, piece, found[c])
            halves_.append(jnp.concatenate(found, axis=0))
        second = jnp.concatenate(halves_, axis=1)
        up = jnp.concatenate(first + ([second[0:sparse]] if sparse else []), axis=0)
        upg_ref[k] = up.astype(BF16)
        rel = second[sparse : sparse + 8] - own_pos
        rel = rel + jnp.where(row8 == 0, shift_ref[pl.ds(k, 1), :], 0.0)
        dist = jnp.sqrt(jnp.sum(rel * rel, axis=0, keepdims=True) + 1.0)
        rel_ref[k] = jnp.where(row8 == 3, dist, rel)
        scaled = (dist - centres) * (1.0 / basis_width)
        basis = jnp.where(k < count, jnp.exp(-(scaled * scaled)), 0.0)
        bas_ref[k] = basis
        b_hi = basis.astype(BF16).astype(F32)
        b_lo = basis - b_hi
        stacked = jnp.concatenate([b_hi, b_lo, b_hi, jnp.zeros_like(b_hi)], axis=0).astype(BF16)
        message = mm(rw3, stacked) * up
        msg_ref[k] = message
        return message, rel

    part = 16
    stride = math.gcd(slots, 16)
    sv_ref[...] = jnp.zeros_like(sv_ref)

    def gather_some(number, carry):
        found = [gather(number * stride + step) for step in range(stride)]
        for first in range(0, channels, part):
            sums = [sv_ref[axis, first : first + part] for axis in range(4)]
            for step in range(stride):
                message = msg_ref[number * stride + step, first : first + part]
                rel = found[step][1]
                sums[0] = sums[0] + message
                for axis in range(3):
                    sums[axis + 1] = sums[axis + 1] + message * rel[axis : axis + 1]
            for axis in range(4):
                sv_ref[axis, first : first + part] = sums[axis]
        return carry

    lax.fori_loop(0, slots // stride, gather_some, 0)

    scalar = sv_ref[0] * message_scale
    vectors = [sv_ref[axis + 1] * (message_scale * vector_scale) for axis in range(3)]
    invariant = scalar + scalar * scalar + (vectors[0] * vectors[0] + vectors[1] * vectors[1] + vectors[2] * vectors[2])
    w_out = w_out_ref[...]
    hidden = feat_ref[...].astype(F32) + mm(w_out, invariant.astype(BF16))
    square = iota((channels, channels), 0) == iota((channels, channels), 1)
    ew = jnp.sum(jnp.where(square, ew_ref[...].astype(F32), 0.0), axis=1, keepdims=True)
    gate = 1.0 / (1.0 + jnp.exp(-hidden))
    eshort_ref[...] = jnp.sum(ew * (hidden * gate), axis=0, keepdims=True)
    d_hidden = ew * (gate * (1.0 + hidden * (1.0 - gate)))
    dh_hi, dh_lo = split2(d_hidden)
    d_inv = (mm_tn(w_out, dh_hi) + mm_tn(w_out, dh_lo)).astype(BF16).astype(F32)
    for axis in range(4):
        factor = (1.0 + 2.0 * scalar) * message_scale if axis == 0 else vectors[axis - 1] * (2.0 * message_scale * vector_scale)
        sv_ref[axis] = d_inv * factor
        svb_ref[axis] = (d_inv * factor).astype(BF16)

    acc_ref[...] = jnp.zeros_like(acc_ref)
    reduce_left = jnp.concatenate([rwt_hi.astype(F32), rwt_lo.astype(F32)], axis=0).astype(BF16)
    chunk = 32

    several = math.gcd(slots, 8)
    wide8 = iota((8, several * atoms), 0)
    centres_wide = wide8.astype(F32) * basis_step

    def scatter(number, total):
        steps = [number * several + step for step in range(several)]

        def side_by_side(pieces):
            return jnp.concatenate(pieces, axis=1)

        right, turned = [], [[] for _ in range(3)]
        for k in steps:
            rel8 = rel_ref[k]
            rel_low = [rel8[axis : axis + 1].astype(BF16) for axis in range(3)]
            turns = [jnp.zeros((8, atoms), F32) for _ in range(3)]
            pulled = []
            for first in range(0, channels, chunk):
                at = slice(first, first + chunk)
                message = msg_ref[k, at, :]
                pull = svb_ref[0, at, :]
                for axis in range(3):
                    pull = pull + svb_ref[axis + 1, at, :] * rel_low[axis]
                    turn = sv_ref[axis + 1, at, :] * message
                    for r in range(0, chunk, 8):
                        turns[axis] = turns[axis] + turn[r : r + 8]
                pulled.append(pull * upg_ref[k, at, :])
            right.append(jnp.concatenate(pulled, axis=0))
            for axis in range(3):
                turned[axis].append(turns[axis])
        sums = mm(reduce_left, side_by_side(right))
        d_basis = sums[0:8] + sums[8:16]
        rel8 = side_by_side([rel_ref[k] for k in steps])
        basis = side_by_side([bas_ref[k] for k in steps])
        dist = rel8[3:4]
        slope = d_basis * basis * ((dist - centres_wide) * (-2.0 / (basis_width * basis_width)))
        d_dist = jnp.sum(slope, axis=0, keepdims=True) / dist
        d_rel = jnp.where(wide8 < 3, d_dist * rel8, 0.0)
        for axis in range(3):
            turn = jnp.sum(side_by_side(turned[axis]), axis=0, keepdims=True)
            d_rel = d_rel + jnp.where(wide8 == axis, turn, 0.0)
        d_hi = d_rel.astype(BF16).astype(F32)
        both = d_hi + pltpu.roll(d_rel - d_hi, 4, 0)
        high = side_by_side([col_ref[pl.ds(k, 1), :] // width for k in steps])
        left = jnp.concatenate([jnp.where(high == block, both, 0.0) for block in range(blocks)], axis=0)
        acc_ref[...] += mm_nt(left.astype(BF16), side_by_side([hot_ref[k] for k in steps]))
        for step in range(several):
            total = total + d_rel[:, step * atoms : (step + 1) * atoms]
        return total

    total = lax.fori_loop(0, slots // several, scatter, jnp.zeros((8, atoms), F32))

    def grad_tile(tile):
        block, piece = divmod(tile, tiles)
        g = acc_ref[block * 8 : block * 8 + 8, piece * 128 : (piece + 1) * 128]
        return g + pltpu.roll(g, 4, 0)

    for tile in range(own_tiles):
        gown_ref[:, tile * 128 : (tile + 1) * 128] = grad_tile(tile) - total[:, tile * 128 : (tile + 1) * 128]

    send_ref[...] = jnp.zeros_like(send_ref)
    left1 = iota((1, 128), 1) < exported
    for u in range(all_tiles - own_tiles):
        g = grad_tile(own_tiles + u)
        swapped = pltpu.roll(g, 64, 1)
        for side in range(2):
            if 2 * u + side >= len(domains):
                continue
            a, b, c = domains[2 * u + side]
            device = lax.rem(places[0] + (a + counts[0]), counts[0]) * counts[1]
            device = (device + lax.rem(places[1] + (b + counts[1]), counts[1])) * counts[2]
            device = device + lax.rem(places[2] + (c + counts[2]), counts[2])
            here, there = (g, swapped) if side == 0 else (swapped, g)
            top = jnp.where(left1, here[0:1], there[1:2])
            bottom = jnp.where(left1, here[2:3], 0.0)
            send_ref[device, :, 0:128] += top
            send_ref[device, :, 128:256] += bottom


def spline(distance):
    outer = jnp.maximum(2.0 - distance, 0.0)
    inner = jnp.maximum(1.0 - distance, 0.0)
    return outer * outer * outer * (1.0 / 6.0) - inner * inner * inner * (4.0 / 6.0)


def weights_of(count, position):
    gap = (iota((count, position.shape[1]), 0) - 1).astype(F32) - position
    return spline(jnp.abs(gap))


def slopes_of(count, position):
    gap = (iota((count, position.shape[1]), 0) - 1).astype(F32) - position
    distance = jnp.abs(gap)
    outer = jnp.maximum(2.0 - distance, 0.0)
    inner = jnp.maximum(1.0 - distance, 0.0)
    size = outer * outer * 0.5 - inner * inner * 2.0
    return jnp.where(gap > 0.0, size, -size)


def spread_kernel(counts, info_ref, rho_ref, plane_ref):
    count_x, count_y, count_z = counts
    atoms = info_ref.shape[2] // 4
    tall = CY * count_y + 8
    rho_ref[...] = jnp.zeros_like(rho_ref)

    def domain(number, slot):
        info = info_ref[number]
        wx = weights_of(16, info[:, 0:atoms]) * info[:, 3 * atoms : 4 * atoms]
        even = weights_of(24, info[:, atoms : 2 * atoms])
        odd = pltpu.roll(even, 4, 0)
        for x in range(0, XL, 2):
            first = x * YW
            here = wx[x : x + 1]
            plane_ref[slot, first : first + 16] = here * even[0:16]
            if x + 1 == XL:
                plane_ref[slot, first + 16 : first + 24] = here * even[16:24]
                continue
            there = wx[x + 1 : x + 2]
            plane_ref[slot, first + 16 : first + 24] = here * even[16:24] + there * odd[0:8]
            plane_ref[slot, first + 24 : first + 40] = there * odd[8:24]
        high, low = split2(weights_of(ZL, info[:, 2 * atoms : 3 * atoms]))
        blank = jnp.zeros((256 - XW, atoms), BF16)
        plane_high, plane_low = [jnp.concatenate([half, blank], axis=0) for half in split2(plane_ref[slot, 0:XW])]
        both = mm_nt(jnp.concatenate([high, low], axis=0), plane_high)
        return both[0:ZL] + both[ZL : 2 * ZL] + mm_nt(high, plane_low)

    def spread(group, carry):
        grown = [domain(group * count_z + l, l % plane_ref.shape[0]) for l in range(count_z)]
        pieces = []
        for l in range(count_z):
            pieces.append(grown[l][0 : ZL - CZ] + grown[l - 1][CZ:ZL])
            pieces.append(grown[l][ZL - CZ : CZ])
        turned = jnp.transpose(jnp.concatenate(pieces, axis=0))
        first = (group // count_y * CX) * tall + (group % count_y) * CY
        for x in range(XL):
            at = pl.ds(pl.multiple_of(first + x * tall, 8), YW)
            rho_ref[at, :] += turned[x * YW : (x + 1) * YW]
        return carry

    lax.fori_loop(0, count_x * count_y, spread, 0, unroll=2)


def times_z(values, table_high, table_low):
    high, low = split2(values)
    return mm(high, table_high) + mm(high, table_low) + mm(low, table_high)


def wave_kernel(
    counts,
    grown_ref,
    hy_ref,
    hzh_ref,
    hzl_ref,
    kx_ref,
    kxo_ref,
    influence_ref,
    back_ref,
    spec_ref,
):
    count_x, count_y, _ = counts
    grid_x, grid_y = CX * count_x, CY * count_y
    tall = grid_y + 8
    place_x = lax.axis_index("gx")
    planes = math.gcd(grid_x, 8)

    def plane(x, wraps):
        def rows(start, count):
            start = pl.multiple_of(start, 8)
            value = grown_ref[pl.ds(start, count), :]
            return value + grown_ref[pl.ds(start + grid_x * tall, count), :] if wraps else value

        start = x * tall
        top = rows(start, 8) + rows(start + grid_y, 8)
        return mm(hy_ref[...], stack3(jnp.concatenate([top, rows(start + 8, grid_y - 8)], axis=0)))

    def along_z(first, turned):
        at = pl.ds(pl.multiple_of(first * grid_y, 8), planes * grid_y)
        spec_ref[at, :] = times_z(jnp.concatenate(turned, axis=0), hzh_ref[...], hzl_ref[...])

    def along_yz(number, carry):
        along_z(number * planes, [plane(number * planes + step, False) for step in range(planes)])
        return carry

    along_z(0, [plane(step, step < 3) for step in range(planes)])
    lax.fori_loop(1, grid_x // planes, along_yz, 0)

    def along_x(octet, carry):
        def part(ref, x):
            return ref[pl.ds(pl.multiple_of(x * grid_y + octet * 8, 8), 8), :]

        values = jnp.concatenate([part(spec_ref, x) for x in range(grid_x)], axis=0)
        factor = jnp.concatenate([part(influence_ref, x) for x in range(grid_x)], axis=0)
        back = mm(kxo_ref[place_x], stack3(mm(kx_ref[...], stack3(values)) * factor))
        for x in range(XL):
            back_ref[pl.ds(pl.multiple_of(x * grid_y + octet * 8, 8), 8), :] = back[x * 8 : (x + 1) * 8]
        return carry

    lax.fori_loop(0, grid_y // 8, along_x, 0, unroll=8)


def field_kernel(counts, back_ref, pq_ref, hyo_ref, hzoh_ref, hzol_ref, out_ref, phi_ref):
    grid_y = CY * counts[1]
    atoms = pq_ref.shape[1]
    place_y, place_z = [lax.axis_index(axis) for axis in MESH_AXES[1:]]
    for x in range(XL):
        turned = mm(hyo_ref[place_y], stack3(back_ref[x * grid_y : (x + 1) * grid_y]))
        phi_ref[x * YL : (x + 1) * YL] = turned[0:YL]

    own = pq_ref[...]
    charge = own[3:4]
    wx, dx = weights_of(16, own[0:1]), slopes_of(16, own[0:1])
    wy, dy = weights_of(YL, own[1:2]), slopes_of(YL, own[1:2])
    wzh, wzl = split2(jnp.concatenate([weights_of(128, own[2:3]), slopes_of(128, own[2:3])], axis=1))
    high, low = split2(times_z(phi_ref[...], hzoh_ref[place_z], hzol_ref[place_z]))
    lines = mm(high, wzh) + mm(high, wzl) + mm(low, wzh)
    potential = jnp.zeros((1, atoms), F32)
    field = [jnp.zeros((1, atoms), F32) for _ in range(3)]
    for x in range(XL):
        flat = lines[x * YL : (x + 1) * YL, 0:atoms]
        steep = lines[x * YL : (x + 1) * YL, atoms : 2 * atoms]
        s0 = jnp.sum(wy * flat, axis=0, keepdims=True)
        sy = jnp.sum(dy * flat, axis=0, keepdims=True)
        sz = jnp.sum(wy * steep, axis=0, keepdims=True)
        here = wx[x : x + 1]
        potential = potential + here * s0
        field[0] = field[0] + dx[x : x + 1] * s0
        field[1] = field[1] + here * sy
        field[2] = field[2] + here * sz
    out_ref[...] = jnp.zeros_like(out_ref)
    for axis in range(3):
        out_ref[axis : axis + 1] = charge * field[axis]
    out_ref[3:4] = 0.5 * charge * potential


def final_kernel(recv_ref, gown_ref, eshort_ref, long_ref, export_ref, forces_ref, energy_ref):
    atoms = gown_ref.shape[1]

    def returned(device, sums):
        return sums + recv_ref[device]

    sums = lax.fori_loop(0, recv_ref.shape[0], returned, jnp.zeros((1, 256), F32), unroll=8)
    energy_ref[...] = eshort_ref[...] + long_ref[3:4]
    row8 = iota((8, 128), 0)
    lines3 = (sums[:, 0:128], pltpu.roll(jnp.broadcast_to(sums[:, 0:128], (8, 128)), 64, 1), sums[:, 128:256])
    lent = jnp.zeros((8, 128), F32)
    for axis in range(3):
        lent = jnp.where(row8 == axis, lines3[axis], lent)
    lent = jnp.where(iota((8, 128), 1) < 64, lent, 0.0)
    export = export_ref[...]
    twice = jnp.concatenate([export, export], axis=1)
    hot = jnp.where(iota((atoms, 128), 0) == twice, 1.0, 0.0).astype(BF16)
    high, low = split2(lent)
    rest = (lent - high.astype(F32) - low.astype(F32)).astype(BF16)
    back = mm_nt(high, hot) + mm_nt(low, hot) + mm_nt(rest, hot)
    for axis in range(3):
        total = long_ref[axis : axis + 1] + gown_ref[axis : axis + 1] + back[axis : axis + 1]
        forces_ref[axis : axis + 1] = -total


def cas_table(extent):
    indices = np.arange(extent)
    angle = (indices[:, None] * indices[None, :] % extent) * (2.0 * np.pi / extent)
    return (np.cos(angle) + np.sin(angle)) / np.sqrt(extent)


def halves(table):
    high = np.asarray(table, np.float32).astype(BF16)
    low = (np.asarray(table, np.float64) - high.astype(np.float64)).astype(np.float32).astype(BF16)
    return high, low


def wide(table):
    high, low = halves(table)
    return np.concatenate([high, high, low], axis=-1)


def wave_squares(extent):
    folded = (np.arange(extent) + extent // 2) % extent - extent // 2
    return (folded * (2.0 * np.pi / extent)) ** 2


def near(*arrays):
    return [pltpu.with_memory_space_constraint(array, pltpu.VMEM) for array in arrays]


def exchange(block, axes, offsets):
    sizes = [lax.axis_size(axis) for axis in axes]
    moves = []
    for source in np.ndindex(*sizes):
        target = [(place + step) % size for place, step, size in zip(source, offsets, sizes)]
        moves.append((int(np.ravel_multi_index(source, sizes)), int(np.ravel_multi_index(target, sizes))))
    return lax.ppermute(block, axes, moves)


def per_device(
    atom_cell,
    atom_frac,
    features,
    ghost_export,
    neighbors,
    neighbor_count,
    w_up,
    radial_weight,
    w_out,
    energy_weight,
    charge_weight,
):
    channels, atoms = features.shape
    exported = ghost_export.shape[0]
    slots = neighbors.shape[1]
    counts = tuple(lax.axis_size(axis) for axis in MESH_AXES)
    count_x, count_y, count_z = counts
    devices = count_x * count_y * count_z
    half = channels // 2
    rows = channels + 16

    record, own, pq, info = pl.pallas_call(
        prep_kernel,
        out_shape=(
            pltpu.VMEM((half + 16, 2 * exported), BF16),
            pltpu.VMEM((rows, atoms), BF16),
            pltpu.VMEM((8, atoms), F32),
            pltpu.VMEM((devices, 1, 4 * atoms), F32),
        ),
        in_specs=[VMEM] * 6,
        out_specs=(VMEM,) * 4,
        scratch_shapes=[pltpu.VMEM((16, atoms), F32)],
        name="prep",
    )(features, atom_cell, atom_frac, ghost_export[None, :], w_up, charge_weight[None, :])

    info = lax.all_to_all(info, MESH_AXES, split_axis=0, concat_axis=0, tiled=True)
    grid_x, grid_y, grid_z = CX * count_x, CY * count_y, CZ * count_z
    cas_x, cas_y, cas_z = cas_table(grid_x), cas_table(grid_y), cas_table(grid_z)
    square = (
        wave_squares(grid_x)[:, None, None] + wave_squares(grid_y)[None, :, None] + wave_squares(grid_z)[None, None, :]
    )
    safe = np.where(square > 0.0, square, 1.0)
    influence = np.where(square > 0.0, 4.0 * math.pi * np.exp(-square / (4.0 * ewald_beta_sq)) / safe, 0.0)
    influence = influence.reshape(grid_x * grid_y, grid_z).astype(np.float32)
    eye = np.eye(8)
    kx = wide(np.kron(cas_x, eye))
    x_rows = (np.arange(count_x)[:, None] * CX + np.arange(XL + 1)[None, :]) % grid_x
    kxo = np.stack([wide(np.kron(cas_x[r], eye)) for r in x_rows])
    y_rows = (np.arange(count_y)[:, None] * CY + np.arange(32)[None, :]) % grid_y
    hyo = np.stack([wide(cas_y[r]) for r in y_rows])
    z_rows = (np.arange(count_z)[:, None] * CZ + np.arange(128)[None, :]) % grid_z
    hzo = [halves(cas_z[:, r] * (np.arange(128) < ZL)[None, :]) for r in z_rows]
    hzoh, hzol = np.stack([t[0] for t in hzo]), np.stack([t[1] for t in hzo])
    hzh, hzl = halves(cas_z)

    grown_shape = ((grid_x + 3) * (grid_y + 8), grid_z)

    block = record[None]
    if count_x <= 2:
        block = jnp.concatenate([block, exchange(block, ("gx",), (1,))], axis=0)
        x_of = (1, 0, 1)
    else:
        sides = [exchange(block, ("gx",), (step,)) for step in (1, -1)]
        block = jnp.concatenate([sides[0], block, sides[1]], axis=0)
        x_of = (0, 1, 2)
    below = exchange(block, ("gy",), (1,))
    above = exchange(block, ("gy",), (-1,))
    grown = pl.pallas_call(
        functools.partial(spread_kernel, counts),
        out_shape=pltpu.VMEM(grown_shape, F32),
        in_specs=[VMEM],
        out_specs=VMEM,
        scratch_shapes=[pltpu.VMEM((count_z, 256, atoms), F32)],
        compiler_params=PARAMS,
        name="spread",
    )(*near(info))
    if SPREAD_EARLY:
        below, above, grown = lax.optimization_barrier((below, above, grown))
    block = jnp.concatenate([below, block, above], axis=0)
    below = exchange(block, ("gz",), (1,))
    above = exchange(block, ("gz",), (-1,))
    if WAVE_EARLY:
        below, above, grown = lax.optimization_barrier((below, above, grown))
    waves = pl.pallas_call(
        functools.partial(wave_kernel, counts),
        out_shape=pltpu.VMEM((XL * grid_y, grid_z), F32),
        in_specs=[VMEM] * 7,
        out_specs=VMEM,
        scratch_shapes=[
            pltpu.VMEM((grid_x * grid_y, grid_z), F32),
        ],
        compiler_params=PARAMS,
        name="wave",
    )(*near(grown, *[jnp.asarray(t) for t in (wide(cas_y), hzh, hzl, kx, kxo, influence)]))

    domains = lent_domains(count_x)
    width = 256
    dense = 112
    all_tiles = -(-(atoms + len(domains) * exported) // 128)
    blocks = -(-all_tiles * 128 // width)
    send, gown, eshort = pl.pallas_call(
        functools.partial(short_kernel, (counts, x_of, exported, dense)),
        out_shape=(
            pltpu.VMEM((devices, 1, 256), F32),
            pltpu.VMEM((8, atoms), F32),
            pltpu.VMEM((1, atoms), F32),
        ),
        in_specs=[VMEM] * 11,
        out_specs=(VMEM,) * 3,
        scratch_shapes=[
            pltpu.VMEM((blocks * dense, width), BF16),
            pltpu.VMEM((channels - dense + 8, all_tiles * 128), F32),
            pltpu.VMEM((slots, width, atoms), BF16),
            pltpu.VMEM((slots, channels, atoms), BF16),
            pltpu.VMEM((slots, channels, atoms), F32),
            pltpu.VMEM((slots, 8, atoms), F32),
            pltpu.VMEM((slots, 8, atoms), F32),
            pltpu.VMEM((4, channels, atoms), F32),
            pltpu.VMEM((4, channels, atoms), BF16),
            pltpu.VMEM((slots, atoms), F32),
            pltpu.VMEM((slots, atoms), jnp.int32),
            pltpu.VMEM((blocks * 8, width), F32),
        ],
        compiler_params=PARAMS,
        name="short",
    )(
        *near(below, block, above, own),
        *near(neighbors.T, neighbor_count[None, :], pq, features),
        *near(radial_weight.T, w_out, energy_weight[None, :]),
    )

    recv = lax.all_to_all(send, MESH_AXES, split_axis=0, concat_axis=0, tiled=True)

    far = pl.pallas_call(
        functools.partial(field_kernel, counts),
        out_shape=pltpu.VMEM((8, atoms), F32),
        in_specs=[VMEM] * 5,
        out_specs=VMEM,
        scratch_shapes=[pltpu.VMEM((XL * YL, grid_z), F32)],
        compiler_params=PARAMS,
        name="field",
    )(*near(waves, pq, jnp.asarray(hyo), jnp.asarray(hzoh), jnp.asarray(hzol)))
    forces, energy = pl.pallas_call(
        final_kernel,
        out_shape=(jax.ShapeDtypeStruct((3, atoms), F32), jax.ShapeDtypeStruct((1, atoms), F32)),
        in_specs=[VMEM] * 5,
        out_specs=(VMEM,) * 2,
        name="final",
    )(*near(recv, gown, eshort, far, ghost_export[None, :]))
    return (forces, energy.reshape(-1))


def solution(mesh):
    spread = ("gx", "gy", "gz")
    in_specs = (
        P(None, spread),
        P(None, spread),
        P(None, spread),
        P(spread),
        P(spread, None),
        P(spread),
        P(),
        P(),
        P(),
        P(),
        P(),
    )
    out_specs = (P(None, spread), P(spread))

    return jax.shard_map(per_device, mesh=mesh, in_specs=in_specs, out_specs=out_specs, check_vma=False)
```
